32 devices in a mesh: sect: 2 (over core), tok: 2 (over x), vocab: 8 (over z, y).
Axes of the slice: x: 2, y: 2, z: 4, core: 2. Of those that a mesh axis runs over, the one named last changes fastest.
Arguments:
- teacher_hidden: bfloat16 [512, 8192], P('tok', 'sect'), may hold values from -6 to 6
- teacher_head: bfloat16 [8192, 4096], P('sect', 'vocab'), may hold values from -0.19921875 to 0.19921875
- student_hidden: bfloat16 [512, 3072], P('tok', 'sect'), may hold values from -6 to 6
- student_head: bfloat16 [3072, 4096], P('sect', 'vocab'), may hold values from -0.328125 to 0.328125
- live_counts: int32 [2], P('tok'), may hold values from 1 to 256, 384 in all
Outputs:
- loss: float32 [], replicated
- head_grad: bfloat16 [3072, 4096], P(('sect', 'tok'), 'vocab')
- hidden_grad: bfloat16 [512, 3072], P(('tok', 'vocab'), 'sect')
The draws below stay inside these ranges and needn't reach their ends.
Inputs may be any that keep to these rules, and one draw needn't show every extreme that they name: Shard k of the tokens has its first live_counts[k] token slots live and the rest empty.
All inputs are finite; a program needn't handle non-finite values.
Results may differ from the reference program's by a relative error of at most 0.0049.
Values may be sent and summed in bfloat16 or wider, within the bound.
A program may use at most 64 MiB of HBM per device.

```python
import math
import jax
import jax.numpy as jnp
import numpy as np

DT = 8192
DS = 3072
TOK_DEV = 256
VOCAB = 4096
TOKENS = 512
N_TOK = 2


def block_levels(rng, dims, shards, low, largest):
    factor_of, own = 1.0, jax.random.fold_in(rng, 6)
    for dim, blocks in shards:
        draws = jnp.exp(jax.random.uniform(jax.random.fold_in(own, dim), (blocks,), jnp.float32, low / len(shards), largest / len(shards)))
        factor_of = factor_of * jnp.repeat(draws, dims[dim] // blocks).reshape([-1 if axis == dim else 1 for axis in range(len(dims))])
    return factor_of


def split_up(number_of, total, bound, lean):
    loads = [(1 << 20) // math.isqrt(grade ** lean) + 1 for grade in range(2, number_of + 1)]
    rest, counts = total - bound - (number_of - 1), [1] * (number_of - 1)
    while rest > 0:
        free = [i for i in range(number_of - 1) if counts[i] < bound]
        pool, remaining = sum([loads[i] for i in free]), rest
        for i in free:
            more = min(bound - counts[i], max(1, remaining * loads[i] // pool), rest)
            counts[i] = counts[i] + more
            rest = rest - more
    return np.array([bound] + counts)


def uneven_parts(key, amount, total, bound, slope):
    if amount == 2:
        one = jax.random.randint(key, (), max(1, total - bound), min(bound, total - 1) + 1)
        return jnp.stack([one, total - one])
    sizes = jnp.asarray(split_up(amount, total, bound, slope), jnp.int32)
    pairs = (amount - 1) // 2
    donor, sink = sizes[1:1 + 2 * pairs:2], sizes[2:2 + 2 * pairs:2]
    slack = jnp.minimum(donor - 1, bound - sink)
    passed = jax.random.randint(jax.random.fold_in(key, 1), (pairs,), 0, 1 << 20) % (slack + 1)
    sizes = sizes.at[1:1 + 2 * pairs:2].set(donor - passed).at[2:2 + 2 * pairs:2].set(sink + passed)
    return sizes[jax.random.permutation(jax.random.fold_in(key, 2), amount)]


def centred(rng, shape, spread, most, split=(), held_as=jnp.bfloat16):
    level = block_levels(rng, shape, split, -0.22, 0.18) if split else 1.0
    entries = jax.random.normal(rng, shape, jnp.float32) * spread * level
    return jnp.minimum(jnp.maximum(entries, -most), most).astype(held_as)


def setup_inputs(seed: int = 0) -> dict:
    streams_of = jax.random.split(jax.random.key(seed), 6)
    teacher_hidden = centred(streams_of[0], (TOKENS, DT), 1.0, 6.0, ((0, 2), (1, 2)))
    teacher_head = centred(streams_of[1], (DT, VOCAB), 0.0331, 0.19921875, ((0, 2), (1, 8)))
    student_hidden = centred(streams_of[2], (TOKENS, DS), 1.0, 6.0, ((0, 2), (1, 2)))
    student_head = centred(streams_of[3], (DS, VOCAB), 0.0541, 0.328125, ((0, 2), (1, 8)))
    live_counts = uneven_parts(streams_of[4], N_TOK, 3 * TOK_DEV * N_TOK // 4, TOK_DEV, 2).astype(jnp.int32)
    return dict(teacher_hidden=teacher_hidden, teacher_head=teacher_head, student_hidden=student_hidden, student_head=student_head, live_counts=live_counts)


def reference(teacher_hidden, teacher_head, student_hidden, student_head, live_counts):
    live_rows = (jnp.arange(TOK_DEV, dtype=jnp.int32)[None, :] < live_counts[:, None]).reshape(TOKENS).astype(jnp.float32)
    live_total = jnp.sum(live_counts.astype(jnp.float32))
    teacher = jnp.dot(teacher_hidden, teacher_head, preferred_element_type=jnp.float32) * 0.5
    student = jnp.dot(student_hidden, student_head, preferred_element_type=jnp.float32) * 0.5
    teacher_exp = jnp.exp(teacher)
    student_exp = jnp.exp(student)
    teacher_sum = jnp.sum(teacher_exp, axis=1)
    student_sum = jnp.sum(student_exp, axis=1)
    cross = jnp.sum(teacher_exp * (teacher - student), axis=1)
    divergence = cross / teacher_sum - jnp.log(teacher_sum) + jnp.log(student_sum)
    loss = jnp.sum(live_rows * divergence) / live_total
    row_scale = live_rows * (32.0 * VOCAB * 0.5 / live_total)
    logit_grad = (row_scale[:, None] * (student_exp / student_sum[:, None] - teacher_exp / teacher_sum[:, None])).astype(jnp.bfloat16)
    head_grad = jnp.dot(student_hidden.T, logit_grad, preferred_element_type=jnp.float32).astype(jnp.bfloat16)
    hidden_grad = jnp.dot(logit_grad, student_head.T, preferred_element_type=jnp.float32).astype(jnp.bfloat16)
    return (loss, head_grad, hidden_grad)
```

```python
import functools

import jax
import jax.numpy as jnp
from jax import lax
from jax.experimental import pallas as pl
from jax.experimental.pallas import tpu as pltpu
from jax.sharding import PartitionSpec as P


def softened(teacher_logits, student_logits):
    teacher = teacher_logits * 0.5
    student = student_logits * 0.5
    teacher_exp = jnp.exp(teacher)
    student_exp = jnp.exp(student)
    partial_sums = (
        jnp.sum(teacher_exp, axis=1),
        jnp.sum(student_exp, axis=1),
        jnp.sum(teacher_exp * (teacher - student), axis=1),
    )
    return (teacher_exp, student_exp, partial_sums)


def finish(teacher_exp, student_exp, totals, live_rows, live_total, vocab_entries):
    teacher_sum, student_sum, cross = totals
    divergence = cross / teacher_sum - jnp.log(teacher_sum) + jnp.log(student_sum)
    numerator = jnp.sum(live_rows * divergence)
    row_scale = live_rows * (32.0 * vocab_entries * 0.5 / live_total)
    logit_grad = (
        row_scale[:, None]
        * (student_exp / student_sum[:, None] - teacher_exp / teacher_sum[:, None])
    ).astype(jnp.bfloat16)
    return (logit_grad, numerator)


def body(teacher_hidden, teacher_head, student_hidden, student_head, live_counts):
    token_rows = teacher_hidden.shape[0]
    vocab_entries = student_head.shape[1] * lax.axis_size("vocab")
    live_total = lax.psum(jnp.sum(live_counts.astype(jnp.float32)), "tok")
    live_rows = (jnp.arange(token_rows, dtype=jnp.int32) < live_counts[0]).astype(jnp.float32)
    teacher_part = jnp.dot(teacher_hidden, teacher_head, preferred_element_type=jnp.float32)
    student_part = jnp.dot(student_hidden, student_head, preferred_element_type=jnp.float32)
    teacher_logits, student_logits = lax.psum((teacher_part, student_part), "sect")
    teacher_exp, student_exp, partial_sums = softened(teacher_logits, student_logits)
    totals = lax.psum((partial_sums[0], partial_sums[1], partial_sums[2]), "vocab")
    logit_grad, numerator = finish(
        teacher_exp, student_exp, totals, live_rows, live_total, vocab_entries
    )
    owned_features = lax.all_to_all(student_hidden, "tok", split_axis=1, concat_axis=0, tiled=True)
    head_sum = lax.dot_general(
        owned_features,
        lax.all_gather(logit_grad, "tok", axis=0, tiled=True),
        (((0,), (0,)), ((), ())),
        preferred_element_type=jnp.float32,
    )
    head_grad = head_sum.astype(jnp.bfloat16)
    hidden_grad = lax.psum_scatter(
        lax.dot_general(
            logit_grad, student_head, (((1,), (1,)), ((), ())), preferred_element_type=jnp.float32
        ),
        "vocab",
        scatter_dimension=0,
        tiled=True,
    ).astype(jnp.bfloat16)
    loss = lax.psum(numerator, "tok") / live_total
    return (loss, head_grad, hidden_grad)


MESH = pl.DeviceIdType.MESH
TILE = 32
F32, BF16 = jnp.float32, jnp.bfloat16


def fused(
    n_tok, n_in, n_out, kc, fw,
    counts, th_hbm, thead_hbm, sh_hbm, shead_hbm,
    loss_ref, head_ref, hid_ref,
    th, thead, sh, shead, spart, tpart, srecv, trecv, te_ref, se_ref, stat, ssend, zrecv,
    cnt, crecv, num, nrecv, hown, hrecv, grad, grecv, head_acc,
    zt_f, zt_b, zt_r, zs_f, zs_b, zs_r, yt_f, yt_b, yt_r, ys_f, ys_b, ys_r,
    load_sem, p_ss, p_rs, c_ss, c_rs, h_ss, h_rs, s_ss, s_rs, g_ss, g_rs, n_ss, n_rs,
    o_ss, o_rs, za_ss, za_rs, zb_ss, zb_rs, ya_ss, ya_rs, yb_ss, yb_rs,
):
    sect, tok, voc = lax.axis_index("sect"), lax.axis_index("tok"), lax.axis_index("vocab")
    _, n_voc, sub, feats = sh.shape
    half, rows, width = n_voc * sub, 2 * n_voc * sub, shead.shape[1]
    steps, y_chunks = th.shape[0], yt_r.shape[1]
    inner, outer = voc % n_in, voc // n_in
    across, oth = 1 - inner, 1 - sect
    out_peers = [(outer + d) % n_out for d in range(1, n_out)]
    block = feats // n_tok
    other = {"sect": oth}
    tok_peers = [(tok + d) % n_tok for d in range(1, n_tok)]
    voc_peers = [(voc + d) % n_voc for d in range(1, n_voc)]
    sum_peers = [(s, (tok + d) % n_tok) for d in range(n_tok) for s in (sect, oth)][1:]

    barrier = pltpu.get_barrier_semaphore()
    for s, p in sum_peers:
        pl.semaphore_signal(
            barrier, inc=1, device_id={"sect": s, "tok": p}, device_id_type=MESH
        )
    for p in voc_peers:
        pl.semaphore_signal(barrier, inc=1, device_id={"vocab": p}, device_id_type=MESH)

    sh_loads = [pltpu.make_async_copy(sh_hbm.at[:, q], sh.at[q], load_sem.at[q]) for q in (0, 1)]
    sh_loads.append(pltpu.make_async_copy(shead_hbm, shead, load_sem.at[2]))
    th_loads = [
        [
            pltpu.make_async_copy(
                th_hbm.at[:, q, :, pl.ds(k * kc, kc)], th.at[k, q], load_sem.at[3 + 3 * k + q]
            )
            for q in (0, 1)
        ]
        + [
            pltpu.make_async_copy(
                thead_hbm.at[pl.ds(k * kc, kc)], thead.at[k], load_sem.at[5 + 3 * k]
            )
        ]
        for k in range(steps)
    ]
    for load in sh_loads + sum(th_loads, []):
        load.start()

    def send(src, dst, ss, rs, to):
        copy = pltpu.make_async_remote_copy(
            src_ref=src, dst_ref=dst, send_sem=ss, recv_sem=rs, device_id=to, device_id_type=MESH
        )
        copy.start()
        return copy

    cnt[...] = jnp.full(cnt.shape, counts[0].astype(F32))
    for load in sh_loads:
        load.wait()
    spart[...] = jnp.dot(
        sh[...].reshape(rows, feats), shead[...], preferred_element_type=F32
    ).reshape(2, half, width)
    pl.semaphore_wait(barrier, len(sum_peers) + n_voc - 1)
    c_cp, h_cp, s_cp, g_cp, n_cp = [], [], [], [], []
    p_cp = [send(spart.at[oth], srecv, p_ss.at[0], p_rs.at[0], other)]
    for i, p in enumerate(tok_peers):
        c_cp.append(send(cnt, crecv.at[i], c_ss.at[i], c_rs.at[i], {"tok": p}))
        cols = pl.ds(pl.multiple_of(p * block, block), block)
        h_cp.append(
            send(sh.at[:, :, :, cols], hrecv.at[i], h_ss.at[i], h_rs.at[i], {"tok": p})
        )
    for k in range(steps):
        for load in th_loads[k]:
            load.wait()
        term = jnp.dot(
            th[k].reshape(rows, kc), thead[k], preferred_element_type=F32
        ).reshape(2, half, width)
        tpart[...] = term if k == 0 else tpart[...] + term
    p_cp.append(send(tpart.at[oth], trecv, p_ss.at[1], p_rs.at[1], other))
    for copy in p_cp:
        copy.wait_recv()

    lane = lax.broadcasted_iota(jnp.int32, (TILE, 128), 1)

    def soften(i, carry):
        at = pl.ds(pl.multiple_of(i * TILE, TILE), TILE)
        s = (spart[sect, at, :] + srecv[at, :]) * 0.5
        t = (tpart[sect, at, :] + trecv[at, :]) * 0.5
        te, se = jnp.exp(t), jnp.exp(s)
        te_ref[at, :] = te
        se_ref[at, :] = se
        zt = jnp.sum(te, axis=1, keepdims=True)
        zs = jnp.sum(se, axis=1, keepdims=True)
        cross = jnp.sum(te * (t - s), axis=1, keepdims=True)
        stat[at, :] = jnp.where(lane == 0, zt, jnp.where(lane == 1, zs, cross))
        return carry

    lax.fori_loop(0, half // TILE, soften, 0)
    ssend[...] = stat[...].T[:4]
    for i, p in enumerate(voc_peers):
        s_cp.append(send(ssend, zrecv.at[i], s_ss.at[i], s_rs.at[i], {"vocab": p}))
    mine_cols = pl.ds(pl.multiple_of(tok * block, block), block)
    hown[...] = sh[:, :, :, mine_cols].reshape(rows, block).T
    for copy in c_cp:
        copy.wait_recv()
    total = cnt[...]
    for i in range(n_tok - 1):
        total = total + crecv[i]
    live_total = total[0:1, 0:1]
    scale = 32.0 * (width * n_voc) * 0.5 / live_total
    place = lax.broadcasted_iota(jnp.int32, (1, half), 1)
    row = (place // sub) * (2 * sub) + sect * sub + place % sub
    live = (row.astype(F32) < cnt[0:1, 0:1]).astype(F32)
    totals = ssend[...]
    for i, copy in enumerate(s_cp):
        copy.wait_recv()
        totals = totals + zrecv[i]
    zt, zs, cross = totals[0:1], totals[1:2], totals[2:3]
    a, b = live * scale / zs, live * scale / zt
    coef = jnp.concatenate([a, b] * 4, axis=0)
    stat[...] = jnp.concatenate([coef] * 16, axis=0).T

    def finish_tile(i, carry):
        at = pl.ds(pl.multiple_of(i * TILE, TILE), TILE)
        c = stat[at, :]
        g = c[:, 0:1] * se_ref[at, :] - c[:, 1:2] * te_ref[at, :]
        grad[sect, at, :] = g.astype(BF16)
        return carry

    lax.fori_loop(0, half // TILE, finish_tile, 0)
    o_cp = send(grad.at[sect], grad.at[sect], o_ss, o_rs, other)

    za_cp, zb_cp, ya_cp, yb_cp = [], [], [], []
    order = [-1] + list(range(y_chunks))

    def terms(j, q):
        g = grad[q]
        for f in order:
            term = lax.dot_general(
                g, shead[(f + 1) * fw:(f + 2) * fw, :], (((1,), (1,)), ((), ())),
                preferred_element_type=F32,
            ).reshape(n_out, n_in, sub, fw)
            if f < 0:
                zt_f[j] = term
                zt_b[j] = term.astype(BF16)
                for i, p in enumerate(out_peers):
                    za_cp.append(
                        send(zt_b.at[j, p], zt_r.at[j, i], za_ss.at[j, i], za_rs.at[j, i],
                             {"vocab": p * n_in + inner})
                    )
            else:
                yt_f[j, f] = term
                yt_b[j, f] = term.astype(BF16)
                ya_cp.append(
                    send(yt_b.at[j, f, :, across], yt_r.at[j, f], ya_ss.at[j, f], ya_rs.at[j, f],
                         {"vocab": outer * n_in + across})
                )

    def send_grad(j, q):
        for i, p in enumerate(tok_peers):
            g_cp.append(send(grad.at[q], grecv.at[i, q], g_ss.at[i, j], g_rs.at[i, j], {"tok": p}))

    terms(0, sect)
    send_grad(0, sect)
    o_cp.wait_recv()
    terms(1, oth)
    send_grad(1, oth)
    kl = cross / zt - jnp.log(zt) + jnp.log(zs)
    num[...] = jnp.broadcast_to(jnp.sum(live * kl, axis=1, keepdims=True), num.shape)
    for i, (s, p) in enumerate(sum_peers):
        n_cp.append(send(num, nrecv.at[i], n_ss.at[i], n_rs.at[i], {"sect": s, "tok": p}))
    head_acc[...] = jnp.dot(
        hown[...], grad[...].reshape(rows, width), preferred_element_type=F32
    )

    def take_z(j):
        part = zt_f[j, outer]
        for i in range(n_out - 1):
            za_cp[j * (n_out - 1) + i].wait_recv()
            part = part + zt_r[j, i].astype(F32)
        zs_f[j] = part
        zs_b[j] = part.astype(BF16)
        yb_cp.append(
            send(zs_b.at[j, across], zs_r.at[j], yb_ss.at[j], yb_rs.at[j],
                 {"vocab": outer * n_in + across})
        )

    def take_y(j, f):
        ya_cp[j * y_chunks + f].wait_recv()
        pair = yt_f[j, f, :, inner] + yt_r[j, f].astype(F32)
        ys_f[j, f] = pair
        ys_b[j, f] = pair.astype(BF16)
        for i, p in enumerate(out_peers):
            zb_cp.append(
                send(ys_b.at[j, f, p], ys_r.at[j, f, i], zb_ss.at[j, f, i], zb_rs.at[j, f, i],
                     {"vocab": p * n_in + inner})
            )

    for j in range(2):
        for f in range(y_chunks):
            take_y(j, f)
            if f == 0:
                take_z(j)

    head = head_acc[...]
    numerator = num[...]
    for i, copy in enumerate(n_cp):
        copy.wait_recv()
        numerator = numerator + nrecv[i]
    for i in range(n_tok - 1):
        h_cp[i].wait_recv()
        theirs = hrecv[i].reshape(rows, block).T
        g_cp[i].wait_recv()
        g_cp[n_tok - 1 + i].wait_recv()
        head = head + jnp.dot(theirs, grecv[i].reshape(rows, width), preferred_element_type=F32)
    head_ref[...] = head.astype(BF16)
    loss_ref[...] = numerator / live_total

    for j, q in ((0, sect), (1, oth)):
        yb_cp[j].wait_recv()
        hid_ref[q, :, 0:fw] = (zs_f[j, inner] + zs_r[j].astype(F32)).astype(BF16)
        for f in range(y_chunks):
            hid = ys_f[j, f, outer]
            for i in range(n_out - 1):
                zb_cp[(j * y_chunks + f) * (n_out - 1) + i].wait_recv()
                hid = hid + ys_r[j, f, i].astype(F32)
            hid_ref[q, :, (f + 1) * fw:(f + 2) * fw] = hid.astype(BF16)
    o_cp.wait_send()
    for copy in p_cp + c_cp + h_cp + s_cp + g_cp + n_cp + za_cp + zb_cp + ya_cp + yb_cp:
        copy.wait_send()


def emit(loss_in, head_in, hid_in, loss_out, head_out, hid_out, sems):
    copies = [
        pltpu.make_async_copy(head_in, head_out, sems.at[0]),
        pltpu.make_async_copy(hid_in, hid_out, sems.at[1]),
    ]
    for copy in copies:
        copy.start()
    loss_out[...] = loss_in[0:1, 0:1]
    for copy in copies:
        copy.wait()


def fused_body(n_tok, n_voc, teacher_hidden, teacher_head, student_hidden, student_head, live_counts):
    rows, t_feats = teacher_hidden.shape
    feats, width = student_head.shape
    kc, fw = t_feats // 4, feats // 4
    block, out_rows, half = feats // n_tok, rows // n_voc, rows // 2
    sub = out_rows // 2
    n_in, n_out = 2, n_voc // 2
    tp, vp, op, sp = n_tok - 1, n_voc - 1, n_out - 1, 2 * n_tok - 1
    steps, ny = t_feats // kc, feats // fw - 1
    vmem, dma = pltpu.VMEM, pltpu.SemaphoreType.DMA
    any_spec = pl.BlockSpec(memory_space=pl.ANY)
    vm_spec = pl.BlockSpec(memory_space=pltpu.VMEM)
    loss, head, hid = pl.pallas_call(
        functools.partial(fused, n_tok, n_in, n_out, kc, fw),
        out_shape=(
            jax.ShapeDtypeStruct((8, 128), F32),
            jax.ShapeDtypeStruct((block, width), BF16),
            jax.ShapeDtypeStruct((2, sub, feats), BF16),
        ),
        in_specs=[pl.BlockSpec(memory_space=pltpu.SMEM)] + [any_spec] * 4,
        out_specs=(vm_spec,) * 3,
        scratch_shapes=[
            vmem((steps, 2, n_voc, sub, kc), BF16), vmem((steps, kc, width), BF16),
            vmem((2, n_voc, sub, feats), BF16), vmem((feats, width), BF16),
            vmem((2, half, width), F32), vmem((2, half, width), F32),
            vmem((half, width), F32), vmem((half, width), F32),
            vmem((half, width), F32), vmem((half, width), F32),
            vmem((half, 128), F32), vmem((4, half), F32), vmem((vp, 4, half), F32),
            vmem((8, 128), F32), vmem((tp, 8, 128), F32),
            vmem((8, 128), F32), vmem((sp, 8, 128), F32),
            vmem((block, rows), BF16), vmem((tp, 2, n_voc, sub, block), BF16),
            vmem((2, half, width), BF16), vmem((tp, 2, half, width), BF16),
            vmem((block, width), F32),
            vmem((2, n_out, n_in, sub, fw), F32), vmem((2, n_out, n_in, sub, fw), BF16),
            vmem((2, op, n_in, sub, fw), BF16),
            vmem((2, n_in, sub, fw), F32), vmem((2, n_in, sub, fw), BF16),
            vmem((2, sub, fw), BF16),
            vmem((2, ny, n_out, n_in, sub, fw), F32), vmem((2, ny, n_out, n_in, sub, fw), BF16),
            vmem((2, ny, n_out, sub, fw), BF16),
            vmem((2, ny, n_out, sub, fw), F32), vmem((2, ny, n_out, sub, fw), BF16),
            vmem((2, ny, op, sub, fw), BF16),
            dma((3 + 3 * steps,)), dma((2,)), dma((2,)), dma((tp,)), dma((tp,)), dma((tp,)), dma((tp,)),
            dma((vp,)), dma((vp,)), dma((tp, 2)), dma((tp, 2)), dma((sp,)), dma((sp,)),
            dma(()), dma(()), dma((2, op)), dma((2, op)), dma((2, ny, op)), dma((2, ny, op)),
            dma((2, ny)), dma((2, ny)), dma((2,)), dma((2,)),
        ],
        compiler_params=pltpu.CompilerParams(
            collective_id=0, has_side_effects=True, vmem_limit_bytes=53 * 1024 * 1024
        ),
    )(
        live_counts, teacher_hidden.reshape(n_voc, 2, sub, t_feats), teacher_head,
        student_hidden.reshape(n_voc, 2, sub, feats), student_head,
    )
    hid = hid.reshape(out_rows, feats)
    loss, head, hid = pl.pallas_call(
        emit,
        out_shape=(
            jax.ShapeDtypeStruct((1, 1), F32),
            jax.ShapeDtypeStruct(head.shape, BF16),
            jax.ShapeDtypeStruct(hid.shape, BF16),
        ),
        in_specs=[vm_spec, any_spec, any_spec],
        out_specs=(vm_spec, any_spec, any_spec),
        scratch_shapes=[dma((2,))],
        compiler_params=pltpu.CompilerParams(vmem_limit_bytes=4 * 1024 * 1024),
    )(loss, head, hid)
    return (loss[0, 0], head, hid)


def solution(mesh):
    placed = (P("tok", "sect"), P("sect", "vocab"), P("tok", "sect"), P("sect", "vocab"), P("tok"))
    n_tok, n_voc = mesh.shape["tok"], mesh.shape["vocab"]

    def run(*args):
        rows = args[0].shape[0]
        fits = rows == 256 and rows % (TILE * n_voc) == 0 and n_voc % 2 == 0 and n_voc > 2
        if fits and n_tok > 1:
            return fused_body(n_tok, n_voc, *args)
        return body(*args)

    return jax.shard_map(
        run,
        mesh=mesh,
        in_specs=placed,
        out_specs=(P(), P(("sect", "tok"), "vocab"), P(("tok", "vocab"), "sect")),
        check_vma=False,
    )
```

```python
import functools

import jax
import jax.numpy as jnp
from jax import lax
from jax.experimental import pallas as pl
from jax.experimental.pallas import tpu as pltpu
from jax.sharding import PartitionSpec as P


def softened(teacher_logits, student_logits):
    teacher = teacher_logits * 0.5
    student = student_logits * 0.5
    teacher_exp = jnp.exp(teacher)
    student_exp = jnp.exp(student)
    partial_sums = (
        jnp.sum(teacher_exp, axis=1),
        jnp.sum(student_exp, axis=1),
        jnp.sum(teacher_exp * (teacher - student), axis=1),
    )
    return (teacher_exp, student_exp, partial_sums)


def finish(teacher_exp, student_exp, totals, live_rows, live_total, vocab_entries):
    teacher_sum, student_sum, cross = totals
    divergence = cross / teacher_sum - jnp.log(teacher_sum) + jnp.log(student_sum)
    numerator = jnp.sum(live_rows * divergence)
    row_scale = live_rows * (32.0 * vocab_entries * 0.5 / live_total)
    logit_grad = (
        row_scale[:, None]
        * (student_exp / student_sum[:, None] - teacher_exp / teacher_sum[:, None])
    ).astype(jnp.bfloat16)
    return (logit_grad, numerator)


def body(teacher_hidden, teacher_head, student_hidden, student_head, live_counts):
    token_rows = teacher_hidden.shape[0]
    vocab_entries = student_head.shape[1] * lax.axis_size("vocab")
    live_total = lax.psum(jnp.sum(live_counts.astype(jnp.float32)), "tok")
    live_rows = (jnp.arange(token_rows, dtype=jnp.int32) < live_counts[0]).astype(jnp.float32)
    teacher_part = jnp.dot(teacher_hidden, teacher_head, preferred_element_type=jnp.float32)
    student_part = jnp.dot(student_hidden, student_head, preferred_element_type=jnp.float32)
    teacher_logits, student_logits = lax.psum((teacher_part, student_part), "sect")
    teacher_exp, student_exp, partial_sums = softened(teacher_logits, student_logits)
    totals = lax.psum((partial_sums[0], partial_sums[1], partial_sums[2]), "vocab")
    logit_grad, numerator = finish(
        teacher_exp, student_exp, totals, live_rows, live_total, vocab_entries
    )
    owned_features = lax.all_to_all(student_hidden, "tok", split_axis=1, concat_axis=0, tiled=True)
    head_sum = lax.dot_general(
        owned_features,
        lax.all_gather(logit_grad, "tok", axis=0, tiled=True),
        (((0,), (0,)), ((), ())),
        preferred_element_type=jnp.float32,
    )
    head_grad = head_sum.astype(jnp.bfloat16)
    hidden_grad = lax.psum_scatter(
        lax.dot_general(
            logit_grad, student_head, (((1,), (1,)), ((), ())), preferred_element_type=jnp.float32
        ),
        "vocab",
        scatter_dimension=0,
        tiled=True,
    ).astype(jnp.bfloat16)
    loss = lax.psum(numerator, "tok") / live_total
    return (loss, head_grad, hidden_grad)


MESH = pl.DeviceIdType.MESH
TILE = 32
F32, BF16 = jnp.float32, jnp.bfloat16


def fused(
    n_tok, n_in, n_out, kc, plans,
    counts, th_hbm, thead_hbm, sh_hbm, shead_hbm,
    loss_ref, head_ref, hid_ref,
    th, thead, sh, shead, spart, tpart, srecv, trecv, te_ref, se_ref, stat, ssend, zrecv,
    cnt, crecv, num, nrecv, hown, hrecv, grad, grecv, head_acc,
    coef, apart, pre_b, pre_r, zt_f, zt_b, zt_r, zs_f, zs_b, zs_r, yt_f, yt_b, yt_r, ys_f, ys_b, ys_r,
    load_sem, p_ss, p_rs, c_ss, c_rs, h_ss, h_rs, s_ss, s_rs, g_ss, g_rs, n_ss, n_rs,
    o_ss, o_rs, za_ss, za_rs, zb_ss, zb_rs, ya_ss, ya_rs, yb_ss, yb_rs, pre_ss, pre_rs,
):
    sect, tok, voc = lax.axis_index("sect"), lax.axis_index("tok"), lax.axis_index("vocab")
    _, n_voc, sub, feats = sh.shape
    half, rows, width = n_voc * sub, 2 * n_voc * sub, shead.shape[1]
    steps = th.shape[0]
    inner, outer = voc % n_in, voc // n_in
    across, oth = 1 - inner, 1 - sect
    out_peers = [(outer + d) % n_out for d in range(1, n_out)]
    block = feats // n_tok
    other = {"sect": oth}
    tok_peers = [(tok + d) % n_tok for d in range(1, n_tok)]
    voc_peers = [(voc + d) % n_voc for d in range(1, n_voc)]
    sum_peers = [(s, (tok + d) % n_tok) for d in range(n_tok) for s in (sect, oth)][1:]

    sh_loads = [pltpu.make_async_copy(sh_hbm.at[:, q], sh.at[q], load_sem.at[q]) for q in (0, 1)]
    sh_loads.append(pltpu.make_async_copy(shead_hbm, shead, load_sem.at[2]))
    th_loads = [
        [
            pltpu.make_async_copy(
                th_hbm.at[:, q, :, pl.ds(k * kc, kc)], th.at[k, q], load_sem.at[3 + 3 * k + q]
            )
            for q in (0, 1)
        ]
        + [
            pltpu.make_async_copy(
                thead_hbm.at[pl.ds(k * kc, kc)], thead.at[k], load_sem.at[5 + 3 * k]
            )
        ]
        for k in range(steps)
    ]
    for load in sh_loads + sum(th_loads, []):
        load.start()
    barrier = pltpu.get_barrier_semaphore()
    for s, p in sum_peers:
        pl.semaphore_signal(
            barrier, inc=1, device_id={"sect": s, "tok": p}, device_id_type=MESH
        )
    for p in voc_peers:
        pl.semaphore_signal(barrier, inc=1, device_id={"vocab": p}, device_id_type=MESH)


    def make(src, dst, ss, rs, to):
        return pltpu.make_async_remote_copy(
            src_ref=src, dst_ref=dst, send_sem=ss, recv_sem=rs, device_id=to, device_id_type=MESH
        )

    def send(*args):
        copy = make(*args)
        copy.start()
        return copy

    cnt[...] = jnp.full(cnt.shape, counts[0].astype(F32))
    for load in sh_loads:
        load.wait()
    spart[...] = jnp.dot(
        sh[...].reshape(rows, feats), shead[...], preferred_element_type=F32
    ).reshape(2, half, width)
    pl.semaphore_wait(barrier, len(sum_peers) + n_voc - 1)
    c_cp, h_cp, s_cp = [], [], []
    p_cp = [send(spart.at[oth], srecv, p_ss.at[0], p_rs.at[0], other)]
    for i, p in enumerate(tok_peers):
        c_cp.append(send(cnt, crecv.at[i], c_ss.at[i], c_rs.at[i], {"tok": p}))
        cols = pl.ds(pl.multiple_of(p * block, block), block)
        h_cp.append(
            send(sh.at[:, :, :, cols], hrecv.at[i], h_ss.at[i], h_rs.at[i], {"tok": p})
        )
    for k in range(steps):
        for load in th_loads[k]:
            load.wait()
        term = jnp.dot(
            th[k].reshape(rows, kc), thead[k], preferred_element_type=F32
        ).reshape(2, half, width)
        tpart[...] = term if k == 0 else tpart[...] + term
    p_cp.append(send(tpart.at[oth], trecv, p_ss.at[1], p_rs.at[1], other))
    for copy in p_cp:
        copy.wait_recv()

    lane = lax.broadcasted_iota(jnp.int32, (TILE, 128), 1)

    def soften(i, carry):
        at = pl.ds(pl.multiple_of(i * TILE, TILE), TILE)
        s = (spart[sect, at, :] + srecv[at, :]) * 0.5
        t = (tpart[sect, at, :] + trecv[at, :]) * 0.5
        te, se = jnp.exp(t), jnp.exp(s)
        te_ref[at, :] = te
        se_ref[at, :] = se
        zt = jnp.sum(te, axis=1, keepdims=True)
        zs = jnp.sum(se, axis=1, keepdims=True)
        cross = jnp.sum(te * (t - s), axis=1, keepdims=True)
        stat[at, :] = jnp.where(lane == 0, zt, jnp.where(lane == 1, zs, cross))
        return carry

    lax.fori_loop(0, half // TILE, soften, 0)
    ssend[...] = stat[...].T[:4]
    for i, p in enumerate(voc_peers):
        s_cp.append(send(ssend, zrecv.at[i], s_ss.at[i], s_rs.at[i], {"vocab": p}))

    def ahead(fa, f):
        w = fa[f]
        return make(
            pre_b.at[f, :, :, :, 0:w], pre_r.at[f, :, :, :, 0:w], pre_ss.at[f], pre_rs.at[f],
            {"vocab": outer * n_in + across},
        )

    def early(fz, fa, n_pre, late):
        if not n_pre:
            return
        for z in range(n_out):
            at = pl.ds(pl.multiple_of((z * n_in + across) * sub, sub), sub)
            zt, zs = stat[at, 0:1], stat[at, 1:2]
            t = te_ref[at, :] * jnp.where(zt > 0, 1.0 / zt, 0.0)
            s = se_ref[at, :] * jnp.where(zs > 0, 1.0 / zs, 0.0)
            apart[0, z] = (s - t).astype(BF16)
            apart[1, z] = t.astype(BF16)
        start = fz
        for f in range(n_pre):
            w = fa[f]
            pre_b[f, :, :, :, 0:w] = lax.dot_general(
                apart[...].reshape(2 * n_out * sub, width), shead[start:start + w, :],
                (((1,), (1,)), ((), ())), preferred_element_type=F32,
            ).reshape(2, n_out, sub, w).astype(BF16)
            ahead(fa, f).start()
            start += w

    mine_cols = pl.ds(pl.multiple_of(tok * block, block), block)
    for core, plan in enumerate(plans):
        pl.when(sect == core)(functools.partial(early, *plan))
    hown[...] = sh[:, :, :, mine_cols].reshape(rows, block).T
    for copy in c_cp:
        copy.wait_recv()
    total = cnt[...]
    for i in range(n_tok - 1):
        total = total + crecv[i]
    live_total = total[0:1, 0:1]
    scale = 32.0 * (width * n_voc) * 0.5 / live_total
    place = lax.broadcasted_iota(jnp.int32, (1, half), 1)
    row = (place // sub) * (2 * sub) + sect * sub + place % sub
    live = (row.astype(F32) < cnt[0:1, 0:1]).astype(F32)
    totals = ssend[...]
    for i, copy in enumerate(s_cp):
        copy.wait_recv()
        totals = totals + zrecv[i]
    zt, zs, cross = totals[0:1], totals[1:2], totals[2:3]
    a, b = live * scale / zs, live * scale / zt
    slot = (voc - (outer * n_in + across) + n_voc) % n_voc - 1
    peer = zrecv[slot]
    ahead_s = a * peer[1:2]
    scales = jnp.concatenate([a, b, ahead_s, ahead_s - b * peer[0:1]] * 2, axis=0)
    coef[...] = jnp.concatenate([scales] * 16, axis=0).T.reshape(n_out, n_in, sub, 128)

    def finish_tile(i, carry):
        at = pl.ds(pl.multiple_of(i * n_in * sub, n_in * sub), n_in * sub)
        c = coef[i].reshape(n_in * sub, 128)
        g = c[:, 0:1] * se_ref[at, :] - c[:, 1:2] * te_ref[at, :]
        grad[sect, i] = g.reshape(n_in, sub, width).astype(BF16)
        return carry

    lax.fori_loop(0, n_out, finish_tile, 0)
    o_cp = send(grad.at[sect], grad.at[sect], o_ss, o_rs, other)

    def spread(fz, fa, n_pre, late):
        zb_cp, yb_cp = {}, {}
        starts = [fz + sum(fa[:f]) for f in range(len(fa))]
        pair, zp = {"vocab": outer * n_in + across}, [{"vocab": p * n_in + inner} for p in out_peers]
        za_cp = {
            (j, i): make(zt_b.at[j, p, :, :, 0:fz], zt_r.at[j, i, :, :, 0:fz],
                         za_ss.at[j, i], za_rs.at[j, i], zp[i])
            for j in range(2) for i, p in enumerate(out_peers) if fz
        }
        ya_cp = {
            (j, f): make(yt_b.at[j, f, :, across, :, 0:w], yt_r.at[j, f, :, :, 0:w],
                         ya_ss.at[j, f], ya_rs.at[j, f], pair)
            for j in range(2) for f, w in enumerate(fa) if j or f >= n_pre
        }

        def product(g, start, size):
            return lax.dot_general(
                g, shead[start:start + size, :], (((1,), (1,)), ((), ())),
                preferred_element_type=F32,
            ).reshape(n_out, n_in, sub, size)

        def z_terms(j, g):
            term = product(g, 0, fz)
            zt_f[j, :, :, :, 0:fz] = term
            zt_b[j, :, :, :, 0:fz] = term.astype(BF16)
            for i in range(n_out - 1):
                za_cp[j, i].start()

        def y_terms(j, g):
            for f, w in enumerate(fa):
                if j == 0 and f < n_pre:
                    continue
                term = product(g, starts[f], w)
                yt_f[j, f, :, :, :, 0:w] = term
                yt_b[j, f, :, :, :, 0:w] = term.astype(BF16)
                ya_cp[j, f].start()

        def terms(j, q):
            g = grad[q].reshape(half, width)
            if fz:
                z_terms(j, g)
            if not late:
                y_terms(j, g)
            for i, p in enumerate(tok_peers):
                g_cp.append(
                    send(grad.at[q], grecv.at[i, q], g_ss.at[i, j], g_rs.at[i, j], {"tok": p})
                )

        def take_z(j):
            part = zt_f[j, outer, :, :, 0:fz]
            for i in range(n_out - 1):
                za_cp[j, i].wait_recv()
                part = part + zt_r[j, i, :, :, 0:fz].astype(F32)
            zs_f[j, :, :, 0:fz] = part
            zs_b[j, :, :, 0:fz] = part.astype(BF16)
            yb_cp[j] = send(
                zs_b.at[j, across, :, 0:fz], zs_r.at[j, :, 0:fz], yb_ss.at[j], yb_rs.at[j], pair
            )

        def take_pre(f):
            w = fa[f]
            ahead(fa, f).wait_recv()
            g = grad[sect, :, inner].reshape(n_out * sub, width)
            own = lax.dot_general(
                g, shead[starts[f]:starts[f] + w, :], (((1,), (1,)), ((), ())),
                preferred_element_type=F32,
            ).reshape(n_out, sub, w)
            c = coef[:, inner]
            both = (
                own
                + c[:, :, 2:3] * pre_r[f, 0, :, :, 0:w].astype(F32)
                + c[:, :, 3:4] * pre_r[f, 1, :, :, 0:w].astype(F32)
            )
            pass_on(0, f, both)

        def take_y(j, f):
            w = fa[f]
            ya_cp[j, f].wait_recv()
            pass_on(j, f, yt_f[j, f, :, inner, :, 0:w] + yt_r[j, f, :, :, 0:w].astype(F32))

        def pass_on(j, f, both):
            w = fa[f]
            ys_f[j, f, :, :, 0:w] = both
            ys_b[j, f, :, :, 0:w] = both.astype(BF16)
            for i, p in enumerate(out_peers):
                zb_cp[j, f, i] = send(
                    ys_b.at[j, f, p, :, 0:w], ys_r.at[j, f, i, :, 0:w],
                    zb_ss.at[j, f, i], zb_rs.at[j, f, i], zp[i],
                )

        g_cp, n_cp = [], []
        terms(0, sect)
        for f in range(n_pre):
            take_pre(f)
        o_cp.wait_recv()
        terms(1, oth)
        kl = cross / zt - jnp.log(zt) + jnp.log(zs)
        num[...] = jnp.broadcast_to(jnp.sum(live * kl, axis=1, keepdims=True), num.shape)
        for i, (s, p) in enumerate(sum_peers):
            n_cp.append(send(num, nrecv.at[i], n_ss.at[i], n_rs.at[i], {"sect": s, "tok": p}))
        head_acc[...] = jnp.dot(
            hown[...], grad[...].reshape(rows, width), preferred_element_type=F32
        )
        if late:
            take_z(0)
            y_terms(0, grad[sect].reshape(half, width))
            y_terms(1, grad[oth].reshape(half, width))
            take_z(1)
        for j in range(2):
            for f in range(len(fa)):
                if j or f >= n_pre:
                    take_y(j, f)
                if fz and f == 0 and not late:
                    take_z(j)

        head = head_acc[...]
        numerator = num[...]
        for i, copy in enumerate(n_cp):
            copy.wait_recv()
            numerator = numerator + nrecv[i]
        for i in range(n_tok - 1):
            h_cp[i].wait_recv()
            theirs = hrecv[i].reshape(rows, block).T
            g_cp[i].wait_recv()
            g_cp[n_tok - 1 + i].wait_recv()
            head = head + jnp.dot(
                theirs, grecv[i].reshape(rows, width), preferred_element_type=F32
            )
        head_ref[...] = head.astype(BF16)
        loss_ref[...] = numerator / live_total

        for j, q in ((0, sect), (1, oth)):
            if fz:
                yb_cp[j].wait_recv()
                mine = zs_f[j, inner, :, 0:fz] + zs_r[j, :, 0:fz].astype(F32)
                hid_ref[q, :, 0:fz] = mine.astype(BF16)
            for f, w in enumerate(fa):
                hid = ys_f[j, f, outer, :, 0:w]
                for i in range(n_out - 1):
                    zb_cp[j, f, i].wait_recv()
                    hid = hid + ys_r[j, f, i, :, 0:w].astype(F32)
                hid_ref[q, :, starts[f]:starts[f] + w] = hid.astype(BF16)
        for copy in g_cp + n_cp:
            copy.wait_send()
        for f in range(n_pre):
            ahead(fa, f).wait_send()
        for group in (za_cp, zb_cp, ya_cp, yb_cp):
            for copy in group.values():
                copy.wait_send()

    for core, plan in enumerate(plans):
        pl.when(sect == core)(functools.partial(spread, *plan))
    o_cp.wait_send()
    for copy in p_cp + c_cp + h_cp + s_cp:
        copy.wait_send()


def emit(loss_in, head_in, hid_in, loss_out, head_out, hid_out, sems):
    copies = [
        pltpu.make_async_copy(head_in, head_out, sems.at[0]),
        pltpu.make_async_copy(hid_in, hid_out, sems.at[1]),
    ]
    for copy in copies:
        copy.start()
    loss_out[...] = loss_in[0:1, 0:1]
    for copy in copies:
        copy.wait()


def fused_body(n_tok, n_voc, teacher_hidden, teacher_head, student_hidden, student_head, live_counts):
    rows, t_feats = teacher_hidden.shape
    feats, width = student_head.shape
    kc = t_feats // 4
    plans = ((0, (512, 512, 512), 1, False), (512, (512, 512), 1, True))
    fz = max(plan[0] for plan in plans)
    fw = max(max(plan[1]) for plan in plans)
    ny = max(len(plan[1]) for plan in plans)
    block, out_rows, half = feats // n_tok, rows // n_voc, rows // 2
    sub = out_rows // 2
    n_in, n_out = 2, n_voc // 2
    tp, vp, op, sp = n_tok - 1, n_voc - 1, n_out - 1, 2 * n_tok - 1
    steps = t_feats // kc
    vmem, dma = pltpu.VMEM, pltpu.SemaphoreType.DMA
    any_spec = pl.BlockSpec(memory_space=pl.ANY)
    vm_spec = pl.BlockSpec(memory_space=pltpu.VMEM)
    loss, head, hid = pl.pallas_call(
        functools.partial(fused, n_tok, n_in, n_out, kc, plans),
        out_shape=(
            jax.ShapeDtypeStruct((8, 128), F32),
            jax.ShapeDtypeStruct((block, width), BF16),
            jax.ShapeDtypeStruct((2, sub, feats), BF16),
        ),
        in_specs=[pl.BlockSpec(memory_space=pltpu.SMEM)] + [any_spec] * 4,
        out_specs=(vm_spec,) * 3,
        scratch_shapes=[
            vmem((steps, 2, n_voc, sub, kc), BF16), vmem((steps, kc, width), BF16),
            vmem((2, n_voc, sub, feats), BF16), vmem((feats, width), BF16),
            vmem((2, half, width), F32), vmem((2, half, width), F32),
            vmem((half, width), F32), vmem((half, width), F32),
            vmem((half, width), F32), vmem((half, width), F32),
            vmem((half, 128), F32), vmem((4, half), F32), vmem((vp, 4, half), F32),
            vmem((8, 128), F32), vmem((tp, 8, 128), F32),
            vmem((8, 128), F32), vmem((sp, 8, 128), F32),
            vmem((block, rows), BF16), vmem((tp, 2, n_voc, sub, block), BF16),
            vmem((2, n_out, n_in, sub, width), BF16), vmem((tp, 2, n_out, n_in, sub, width), BF16),
            vmem((block, width), F32),
            vmem((n_out, n_in, sub, 128), F32), vmem((2, n_out, sub, width), BF16),
            vmem((ny, 2, n_out, sub, fw), BF16), vmem((ny, 2, n_out, sub, fw), BF16),
            vmem((2, n_out, n_in, sub, fz), F32), vmem((2, n_out, n_in, sub, fz), BF16),
            vmem((2, op, n_in, sub, fz), BF16),
            vmem((2, n_in, sub, fz), F32), vmem((2, n_in, sub, fz), BF16),
            vmem((2, sub, fz), BF16),
            vmem((2, ny, n_out, n_in, sub, fw), F32), vmem((2, ny, n_out, n_in, sub, fw), BF16),
            vmem((2, ny, n_out, sub, fw), BF16),
            vmem((2, ny, n_out, sub, fw), F32), vmem((2, ny, n_out, sub, fw), BF16),
            vmem((2, ny, op, sub, fw), BF16),
            dma((3 + 3 * steps,)), dma((2,)), dma((2,)), dma((tp,)), dma((tp,)), dma((tp,)), dma((tp,)),
            dma((vp,)), dma((vp,)), dma((tp, 2)), dma((tp, 2)), dma((sp,)), dma((sp,)),
            dma(()), dma(()), dma((2, op)), dma((2, op)), dma((2, ny, op)), dma((2, ny, op)),
            dma((2, ny)), dma((2, ny)), dma((2,)), dma((2,)), dma((ny,)), dma((ny,)),
        ],
        compiler_params=pltpu.CompilerParams(
            collective_id=0, has_side_effects=True, vmem_limit_bytes=53 * 1024 * 1024
        ),
    )(
        live_counts, teacher_hidden.reshape(n_voc, 2, sub, t_feats), teacher_head,
        student_hidden.reshape(n_voc, 2, sub, feats), student_head,
    )
    hid = hid.reshape(out_rows, feats)
    loss, head, hid = pl.pallas_call(
        emit,
        out_shape=(
            jax.ShapeDtypeStruct((1, 1), F32),
            jax.ShapeDtypeStruct(head.shape, BF16),
            jax.ShapeDtypeStruct(hid.shape, BF16),
        ),
        in_specs=[vm_spec, any_spec, any_spec],
        out_specs=(vm_spec, any_spec, any_spec),
        scratch_shapes=[dma((2,))],
        compiler_params=pltpu.CompilerParams(vmem_limit_bytes=4 * 1024 * 1024),
    )(loss, head, hid)
    return (loss[0, 0], head, hid)


def solution(mesh):
    placed = (P("tok", "sect"), P("sect", "vocab"), P("tok", "sect"), P("sect", "vocab"), P("tok"))
    n_tok, n_voc = mesh.shape["tok"], mesh.shape["vocab"]

    def run(*args):
        rows = args[0].shape[0]
        fits = rows == 256 and rows % (TILE * n_voc) == 0 and n_voc % 2 == 0 and n_voc > 2
        if fits and n_tok > 1:
            return fused_body(n_tok, n_voc, *args)
        return body(*args)

    return jax.shard_map(
        run,
        mesh=mesh,
        in_specs=placed,
        out_specs=(P(), P(("sect", "tok"), "vocab"), P(("tok", "vocab"), "sect")),
        check_vma=False,
    )
```

```python
import functools

import jax
import jax.numpy as jnp
from jax import lax
from jax.experimental import pallas as pl
from jax.experimental.pallas import tpu as pltpu
from jax.sharding import PartitionSpec as P


def softened(teacher_logits, student_logits):
    teacher = teacher_logits * 0.5
    student = student_logits * 0.5
    teacher_exp = jnp.exp(teacher)
    student_exp = jnp.exp(student)
    partial_sums = (
        jnp.sum(teacher_exp, axis=1),
        jnp.sum(student_exp, axis=1),
        jnp.sum(teacher_exp * (teacher - student), axis=1),
    )
    return (teacher_exp, student_exp, partial_sums)


def finish(teacher_exp, student_exp, totals, live_rows, live_total, vocab_entries):
    teacher_sum, student_sum, cross = totals
    divergence = cross / teacher_sum - jnp.log(teacher_sum) + jnp.log(student_sum)
    numerator = jnp.sum(live_rows * divergence)
    row_scale = live_rows * (32.0 * vocab_entries * 0.5 / live_total)
    logit_grad = (
        row_scale[:, None]
        * (student_exp / student_sum[:, None] - teacher_exp / teacher_sum[:, None])
    ).astype(jnp.bfloat16)
    return (logit_grad, numerator)


def body(teacher_hidden, teacher_head, student_hidden, student_head, live_counts):
    token_rows = teacher_hidden.shape[0]
    vocab_entries = student_head.shape[1] * lax.axis_size("vocab")
    live_total = lax.psum(jnp.sum(live_counts.astype(jnp.float32)), "tok")
    live_rows = (jnp.arange(token_rows, dtype=jnp.int32) < live_counts[0]).astype(jnp.float32)
    teacher_part = jnp.dot(teacher_hidden, teacher_head, preferred_element_type=jnp.float32)
    student_part = jnp.dot(student_hidden, student_head, preferred_element_type=jnp.float32)
    teacher_logits, student_logits = lax.psum((teacher_part, student_part), "sect")
    teacher_exp, student_exp, partial_sums = softened(teacher_logits, student_logits)
    totals = lax.psum((partial_sums[0], partial_sums[1], partial_sums[2]), "vocab")
    logit_grad, numerator = finish(
        teacher_exp, student_exp, totals, live_rows, live_total, vocab_entries
    )
    owned_features = lax.all_to_all(student_hidden, "tok", split_axis=1, concat_axis=0, tiled=True)
    head_sum = lax.dot_general(
        owned_features,
        lax.all_gather(logit_grad, "tok", axis=0, tiled=True),
        (((0,), (0,)), ((), ())),
        preferred_element_type=jnp.float32,
    )
    head_grad = head_sum.astype(jnp.bfloat16)
    hidden_grad = lax.psum_scatter(
        lax.dot_general(
            logit_grad, student_head, (((1,), (1,)), ((), ())), preferred_element_type=jnp.float32
        ),
        "vocab",
        scatter_dimension=0,
        tiled=True,
    ).astype(jnp.bfloat16)
    loss = lax.psum(numerator, "tok") / live_total
    return (loss, head_grad, hidden_grad)


MESH = pl.DeviceIdType.MESH
TILE = 32
F32, BF16 = jnp.float32, jnp.bfloat16


def fused(
    n_tok, n_in, n_out, kc, plans,
    counts, th_hbm, thead_hbm, sh_hbm, shead_hbm,
    loss_ref, head_ref, hid_ref,
    th, thead, sh, shead, turned, spart, tpart, srecv, trecv, te_ref, se_ref, stat, ssend, zrecv,
    cnt, crecv, num, nrecv, hown, hrecv, grad, grecv, head_acc,
    coef, apart, pre_b, pre_r, zt_f, zt_b, zt_r, zs_f, zs_b, zs_r, yt_f, yt_b, yt_r, ys_f, ys_b, ys_r,
    load_sem, p_ss, p_rs, c_ss, c_rs, h_ss, h_rs, s_ss, s_rs, g_ss, g_rs, n_ss, n_rs,
    o_ss, o_rs, za_ss, za_rs, zb_ss, zb_rs, ya_ss, ya_rs, yb_ss, yb_rs, pre_ss, pre_rs,
):
    sect, tok, voc = lax.axis_index("sect"), lax.axis_index("tok"), lax.axis_index("vocab")
    _, n_voc, sub, feats = sh.shape
    half, rows, width = n_voc * sub, 2 * n_voc * sub, shead.shape[1]
    steps = th.shape[0]
    inner, outer = voc % n_in, voc // n_in
    across, oth = 1 - inner, 1 - sect
    out_peers = [(outer + d) % n_out for d in range(1, n_out)]
    block = feats // n_tok
    other = {"sect": oth}
    tok_peers = [(tok + d) % n_tok for d in range(1, n_tok)]
    voc_peers = [(voc + d) % n_voc for d in range(1, n_voc)]
    sum_peers = [(s, (tok + d) % n_tok) for d in range(n_tok) for s in (sect, oth)][1:]

    sh_loads = [pltpu.make_async_copy(sh_hbm.at[:, q], sh.at[q], load_sem.at[q]) for q in (0, 1)]
    sh_loads.append(pltpu.make_async_copy(shead_hbm, shead, load_sem.at[2]))
    th_loads = [
        [
            pltpu.make_async_copy(
                th_hbm.at[:, q, :, pl.ds(k * kc, kc)], th.at[k, q], load_sem.at[3 + 3 * k + q]
            )
            for q in (0, 1)
        ]
        + [
            pltpu.make_async_copy(
                thead_hbm.at[pl.ds(k * kc, kc)], thead.at[k], load_sem.at[5 + 3 * k]
            )
        ]
        for k in range(steps)
    ]
    for load in sh_loads + sum(th_loads, []):
        load.start()
    barrier = pltpu.get_barrier_semaphore()
    for s, p in sum_peers:
        pl.semaphore_signal(
            barrier, inc=1, device_id={"sect": s, "tok": p}, device_id_type=MESH
        )
    for p in voc_peers:
        pl.semaphore_signal(barrier, inc=1, device_id={"vocab": p}, device_id_type=MESH)


    def make(src, dst, ss, rs, to):
        return pltpu.make_async_remote_copy(
            src_ref=src, dst_ref=dst, send_sem=ss, recv_sem=rs, device_id=to, device_id_type=MESH
        )

    def send(*args):
        copy = make(*args)
        copy.start()
        return copy

    cnt[...] = jnp.full(cnt.shape, counts[0].astype(F32))
    for load in sh_loads:
        load.wait()
    spart[...] = jnp.dot(
        sh[...].reshape(rows, feats), shead[...], preferred_element_type=F32
    ).reshape(2, half, width)
    pl.semaphore_wait(barrier, len(sum_peers) + n_voc - 1)
    c_cp, h_cp, s_cp = [], [], []
    p_cp = [send(spart.at[oth], srecv, p_ss.at[0], p_rs.at[0], other)]
    for i, p in enumerate(tok_peers):
        c_cp.append(send(cnt, crecv.at[i], c_ss.at[i], c_rs.at[i], {"tok": p}))
        cols = pl.ds(pl.multiple_of(p * block, block), block)
        h_cp.append(
            send(sh.at[:, :, :, cols], hrecv.at[i], h_ss.at[i], h_rs.at[i], {"tok": p})
        )
    for k in range(steps):
        for load in th_loads[k]:
            load.wait()
        if k < steps - 1:
            term = jnp.dot(
                th[k].reshape(rows, kc), thead[k], preferred_element_type=F32
            ).reshape(2, half, width)
            tpart[...] = term if k == 0 else tpart[...] + term
            continue
        for q in (oth, sect):
            tpart[q] = tpart[q] + jnp.dot(
                th[k, q].reshape(half, kc), thead[k], preferred_element_type=F32
            )
            if q is oth:
                p_cp.append(send(tpart.at[oth], trecv, p_ss.at[1], p_rs.at[1], other))
    for copy in p_cp:
        copy.wait_recv()

    lane = lax.broadcasted_iota(jnp.int32, (TILE, 128), 1)

    def soften(i, carry):
        at = pl.ds(pl.multiple_of(i * TILE, TILE), TILE)
        s = (spart[sect, at, :] + srecv[at, :]) * 0.5
        t = (tpart[sect, at, :] + trecv[at, :]) * 0.5
        te, se = jnp.exp(t), jnp.exp(s)
        te_ref[at, :] = te
        se_ref[at, :] = se
        zt = jnp.sum(te, axis=1, keepdims=True)
        zs = jnp.sum(se, axis=1, keepdims=True)
        cross = jnp.sum(te * (t - s), axis=1, keepdims=True)
        stat[at, :] = jnp.where(lane == 0, zt, jnp.where(lane == 1, zs, cross))
        return carry

    lax.fori_loop(0, half // TILE, soften, 0)
    ssend[...] = stat[...].T[:4]
    for i, p in enumerate(voc_peers):
        s_cp.append(send(ssend, zrecv.at[i], s_ss.at[i], s_rs.at[i], {"vocab": p}))

    def ahead(fa, f):
        w = fa[f]
        return make(
            pre_b.at[f, :, :, :, 0:w], pre_r.at[f, :, :, :, 0:w], pre_ss.at[f], pre_rs.at[f],
            {"vocab": outer * n_in + across},
        )

    def early(fz, fa, n_pre, late):
        if not n_pre:
            return
        for z in range(n_out):
            at = pl.ds(pl.multiple_of((z * n_in + across) * sub, sub), sub)
            zt, zs = stat[at, 0:1], stat[at, 1:2]
            t = te_ref[at, :] * jnp.where(zt > 0, 1.0 / zt, 0.0)
            s = se_ref[at, :] * jnp.where(zs > 0, 1.0 / zs, 0.0)
            apart[0, z] = (s - t).astype(BF16)
            apart[1, z] = t.astype(BF16)
        start = fz
        for f in range(n_pre):
            w = fa[f]
            pre_b[f, :, :, :, 0:w] = jnp.dot(
                apart[...].reshape(2 * n_out * sub, width), turned[:, start:start + w],
                preferred_element_type=F32,
            ).reshape(2, n_out, sub, w).astype(BF16)
            ahead(fa, f).start()
            start += w

    mine_cols = pl.ds(pl.multiple_of(tok * block, block), block)
    turned[...] = shead[...].T
    for core, plan in enumerate(plans):
        pl.when(sect == core)(functools.partial(early, *plan))
    hown[...] = sh[:, :, :, mine_cols].reshape(rows, block).T
    for copy in c_cp:
        copy.wait_recv()
    total = cnt[...]
    for i in range(n_tok - 1):
        total = total + crecv[i]
    live_total = total[0:1, 0:1]
    scale = 32.0 * (width * n_voc) * 0.5 / live_total
    place = lax.broadcasted_iota(jnp.int32, (1, half), 1)
    row = (place // sub) * (2 * sub) + sect * sub + place % sub
    live = (row.astype(F32) < cnt[0:1, 0:1]).astype(F32)
    totals = ssend[...]
    for i, copy in enumerate(s_cp):
        copy.wait_recv()
        totals = totals + zrecv[i]
    zt, zs, cross = totals[0:1], totals[1:2], totals[2:3]
    a, b = live * scale / zs, live * scale / zt
    slot = (voc - (outer * n_in + across) + n_voc) % n_voc - 1
    peer = zrecv[slot]
    ahead_s = a * peer[1:2]
    scales = jnp.concatenate([a, b, ahead_s, ahead_s - b * peer[0:1]] * 2, axis=0)
    coef[...] = jnp.concatenate([scales] * 16, axis=0).T.reshape(n_out, n_in, sub, 128)

    def finish_tile(i, carry):
        at = pl.ds(pl.multiple_of(i * n_in * sub, n_in * sub), n_in * sub)
        c = coef[i].reshape(n_in * sub, 128)
        g = c[:, 0:1] * se_ref[at, :] - c[:, 1:2] * te_ref[at, :]
        grad[sect, i] = g.reshape(n_in, sub, width).astype(BF16)
        return carry

    lax.fori_loop(0, n_out, finish_tile, 0)
    o_cp = send(grad.at[sect], grad.at[sect], o_ss, o_rs, other)

    def spread(fz, fa, n_pre, late):
        zb_cp, yb_cp = {}, {}
        starts = [fz + sum(fa[:f]) for f in range(len(fa))]
        pair, zp = {"vocab": outer * n_in + across}, [{"vocab": p * n_in + inner} for p in out_peers]
        za_cp = {
            (j, i): make(zt_b.at[j, p, :, :, 0:fz], zt_r.at[j, i, :, :, 0:fz],
                         za_ss.at[j, i], za_rs.at[j, i], zp[i])
            for j in range(2) for i, p in enumerate(out_peers) if fz
        }
        ya_cp = {
            (j, f): make(yt_b.at[j, f, :, across, :, 0:w], yt_r.at[j, f, :, :, 0:w],
                         ya_ss.at[j, f], ya_rs.at[j, f], pair)
            for j in range(2) for f, w in enumerate(fa) if j or f >= n_pre
        }

        def product(g, start, size):
            return jnp.dot(
                g, turned[:, start:start + size], preferred_element_type=F32
            ).reshape(n_out, n_in, sub, size)

        def z_terms(j, g):
            term = product(g, 0, fz)
            zt_f[j, :, :, :, 0:fz] = term
            zt_b[j, :, :, :, 0:fz] = term.astype(BF16)
            for i in range(n_out - 1):
                za_cp[j, i].start()

        def y_terms(j, g):
            for f, w in enumerate(fa):
                if j == 0 and f < n_pre:
                    continue
                term = product(g, starts[f], w)
                yt_f[j, f, :, :, :, 0:w] = term
                yt_b[j, f, :, :, :, 0:w] = term.astype(BF16)
                ya_cp[j, f].start()

        def terms(j, q):
            g = grad[q].reshape(half, width)
            if fz:
                z_terms(j, g)
            if not late:
                y_terms(j, g)
            for i, p in enumerate(tok_peers):
                g_cp.append(
                    send(grad.at[q], grecv.at[i, q], g_ss.at[i, j], g_rs.at[i, j], {"tok": p})
                )

        def take_z(j):
            part = zt_f[j, outer, :, :, 0:fz]
            for i in range(n_out - 1):
                za_cp[j, i].wait_recv()
                part = part + zt_r[j, i, :, :, 0:fz].astype(F32)
            zs_f[j, :, :, 0:fz] = part
            zs_b[j, :, :, 0:fz] = part.astype(BF16)
            yb_cp[j] = send(
                zs_b.at[j, across, :, 0:fz], zs_r.at[j, :, 0:fz], yb_ss.at[j], yb_rs.at[j], pair
            )

        def take_pre(f):
            w = fa[f]
            ahead(fa, f).wait_recv()
            g = grad[sect, :, inner].reshape(n_out * sub, width)
            own = jnp.dot(
                g, turned[:, starts[f]:starts[f] + w], preferred_element_type=F32
            ).reshape(n_out, sub, w)
            c = coef[:, inner]
            both = (
                own
                + c[:, :, 2:3] * pre_r[f, 0, :, :, 0:w].astype(F32)
                + c[:, :, 3:4] * pre_r[f, 1, :, :, 0:w].astype(F32)
            )
            pass_on(0, f, both)

        def take_y(j, f):
            w = fa[f]
            ya_cp[j, f].wait_recv()
            pass_on(j, f, yt_f[j, f, :, inner, :, 0:w] + yt_r[j, f, :, :, 0:w].astype(F32))

        def pass_on(j, f, both):
            w = fa[f]
            ys_f[j, f, :, :, 0:w] = both
            ys_b[j, f, :, :, 0:w] = both.astype(BF16)
            for i, p in enumerate(out_peers):
                zb_cp[j, f, i] = send(
                    ys_b.at[j, f, p, :, 0:w], ys_r.at[j, f, i, :, 0:w],
                    zb_ss.at[j, f, i], zb_rs.at[j, f, i], zp[i],
                )

        g_cp, n_cp = [], []
        terms(0, sect)
        o_cp.wait_recv()
        terms(1, oth)
        for f in range(n_pre):
            take_pre(f)
        kl = cross / zt - jnp.log(zt) + jnp.log(zs)
        num[...] = jnp.broadcast_to(jnp.sum(live * kl, axis=1, keepdims=True), num.shape)
        for i, (s, p) in enumerate(sum_peers):
            n_cp.append(send(num, nrecv.at[i], n_ss.at[i], n_rs.at[i], {"sect": s, "tok": p}))
        head_acc[...] = jnp.dot(
            hown[...], grad[...].reshape(rows, width), preferred_element_type=F32
        )
        if late:
            take_z(0)
            y_terms(0, grad[sect].reshape(half, width))
            y_terms(1, grad[oth].reshape(half, width))
            take_z(1)
        for j in range(2):
            for f in range(len(fa)):
                if j or f >= n_pre:
                    take_y(j, f)
                if fz and f == 0 and not late:
                    take_z(j)

        head = head_acc[...]
        numerator = num[...]
        for i, copy in enumerate(n_cp):
            copy.wait_recv()
            numerator = numerator + nrecv[i]
        for i in range(n_tok - 1):
            h_cp[i].wait_recv()
            theirs = hrecv[i].reshape(rows, block).T
            g_cp[i].wait_recv()
            g_cp[n_tok - 1 + i].wait_recv()
            head = head + jnp.dot(
                theirs, grecv[i].reshape(rows, width), preferred_element_type=F32
            )
        head_ref[...] = head.astype(BF16)
        loss_ref[...] = numerator / live_total

        for j, q in ((0, sect), (1, oth)):
            if fz:
                yb_cp[j].wait_recv()
                mine = zs_f[j, inner, :, 0:fz] + zs_r[j, :, 0:fz].astype(F32)
                hid_ref[q, :, 0:fz] = mine.astype(BF16)
            for f, w in enumerate(fa):
                hid = ys_f[j, f, outer, :, 0:w]
                for i in range(n_out - 1):
                    zb_cp[j, f, i].wait_recv()
                    hid = hid + ys_r[j, f, i, :, 0:w].astype(F32)
                hid_ref[q, :, starts[f]:starts[f] + w] = hid.astype(BF16)
        for copy in g_cp + n_cp:
            copy.wait_send()
        for f in range(n_pre):
            ahead(fa, f).wait_send()
        for group in (za_cp, zb_cp, ya_cp, yb_cp):
            for copy in group.values():
                copy.wait_send()

    for core, plan in enumerate(plans):
        pl.when(sect == core)(functools.partial(spread, *plan))
    o_cp.wait_send()
    for copy in p_cp + c_cp + h_cp + s_cp:
        copy.wait_send()


def emit(loss_in, head_in, hid_in, loss_out, head_out, hid_out, sems):
    copies = [
        pltpu.make_async_copy(head_in, head_out, sems.at[0]),
        pltpu.make_async_copy(hid_in, hid_out, sems.at[1]),
    ]
    for copy in copies:
        copy.start()
    loss_out[...] = loss_in[0:1, 0:1]
    for copy in copies:
        copy.wait()


def fused_body(n_tok, n_voc, teacher_hidden, teacher_head, student_hidden, student_head, live_counts):
    rows, t_feats = teacher_hidden.shape
    feats, width = student_head.shape
    kc = t_feats // 4
    third = feats // 3
    plans = ((0, (third,) * 3, 2, False), (third, (third,) * 2, 1, True))
    fz = max(plan[0] for plan in plans)
    fw = max(max(plan[1]) for plan in plans)
    ny = max(len(plan[1]) for plan in plans)
    block, out_rows, half = feats // n_tok, rows // n_voc, rows // 2
    sub = out_rows // 2
    n_in, n_out = 2, n_voc // 2
    tp, vp, op, sp = n_tok - 1, n_voc - 1, n_out - 1, 2 * n_tok - 1
    steps = t_feats // kc
    vmem, dma = pltpu.VMEM, pltpu.SemaphoreType.DMA
    any_spec = pl.BlockSpec(memory_space=pl.ANY)
    vm_spec = pl.BlockSpec(memory_space=pltpu.VMEM)
    loss, head, hid = pl.pallas_call(
        functools.partial(fused, n_tok, n_in, n_out, kc, plans),
        out_shape=(
            jax.ShapeDtypeStruct((8, 128), F32),
            jax.ShapeDtypeStruct((block, width), BF16),
            jax.ShapeDtypeStruct((2, sub, feats), BF16),
        ),
        in_specs=[pl.BlockSpec(memory_space=pltpu.SMEM)] + [any_spec] * 4,
        out_specs=(vm_spec,) * 3,
        scratch_shapes=[
            vmem((steps, 2, n_voc, sub, kc), BF16), vmem((steps, kc, width), BF16),
            vmem((2, n_voc, sub, feats), BF16), vmem((feats, width), BF16), vmem((width, feats), BF16),
            vmem((2, half, width), F32), vmem((2, half, width), F32),
            vmem((half, width), F32), vmem((half, width), F32),
            vmem((half, width), F32), vmem((half, width), F32),
            vmem((half, 128), F32), vmem((4, half), F32), vmem((vp, 4, half), F32),
            vmem((8, 128), F32), vmem((tp, 8, 128), F32),
            vmem((8, 128), F32), vmem((sp, 8, 128), F32),
            vmem((block, rows), BF16), vmem((tp, 2, n_voc, sub, block), BF16),
            vmem((2, n_out, n_in, sub, width), BF16), vmem((tp, 2, n_out, n_in, sub, width), BF16),
            vmem((block, width), F32),
            vmem((n_out, n_in, sub, 128), F32), vmem((2, n_out, sub, width), BF16),
            vmem((ny, 2, n_out, sub, fw), BF16), vmem((ny, 2, n_out, sub, fw), BF16),
            vmem((2, n_out, n_in, sub, fz), F32), vmem((2, n_out, n_in, sub, fz), BF16),
            vmem((2, op, n_in, sub, fz), BF16),
            vmem((2, n_in, sub, fz), F32), vmem((2, n_in, sub, fz), BF16),
            vmem((2, sub, fz), BF16),
            vmem((2, ny, n_out, n_in, sub, fw), F32), vmem((2, ny, n_out, n_in, sub, fw), BF16),
            vmem((2, ny, n_out, sub, fw), BF16),
            vmem((2, ny, n_out, sub, fw), F32), vmem((2, ny, n_out, sub, fw), BF16),
            vmem((2, ny, op, sub, fw), BF16),
            dma((3 + 3 * steps,)), dma((2,)), dma((2,)), dma((tp,)), dma((tp,)), dma((tp,)), dma((tp,)),
            dma((vp,)), dma((vp,)), dma((tp, 2)), dma((tp, 2)), dma((sp,)), dma((sp,)),
            dma(()), dma(()), dma((2, op)), dma((2, op)), dma((2, ny, op)), dma((2, ny, op)),
            dma((2, ny)), dma((2, ny)), dma((2,)), dma((2,)), dma((ny,)), dma((ny,)),
        ],
        compiler_params=pltpu.CompilerParams(
            collective_id=0, has_side_effects=True, vmem_limit_bytes=53 * 1024 * 1024
        ),
    )(
        live_counts, teacher_hidden.reshape(n_voc, 2, sub, t_feats), teacher_head,
        student_hidden.reshape(n_voc, 2, sub, feats), student_head,
    )
    hid = hid.reshape(out_rows, feats)
    loss, head, hid = pl.pallas_call(
        emit,
        out_shape=(
            jax.ShapeDtypeStruct((1, 1), F32),
            jax.ShapeDtypeStruct(head.shape, BF16),
            jax.ShapeDtypeStruct(hid.shape, BF16),
        ),
        in_specs=[vm_spec, any_spec, any_spec],
        out_specs=(vm_spec, any_spec, any_spec),
        scratch_shapes=[dma((2,))],
        compiler_params=pltpu.CompilerParams(vmem_limit_bytes=4 * 1024 * 1024),
    )(loss, head, hid)
    return (loss[0, 0], head, hid)


def solution(mesh):
    placed = (P("tok", "sect"), P("sect", "vocab"), P("tok", "sect"), P("sect", "vocab"), P("tok"))
    n_tok, n_voc = mesh.shape["tok"], mesh.shape["vocab"]

    def run(*args):
        rows = args[0].shape[0]
        fits = rows == 256 and rows % (TILE * n_voc) == 0 and n_voc % 2 == 0 and n_voc > 2
        fits = fits and args[2].shape[1] % (384 * n_tok) == 0
        if fits and n_tok > 1:
            return fused_body(n_tok, n_voc, *args)
        return body(*args)

    return jax.shard_map(
        run,
        mesh=mesh,
        in_specs=placed,
        out_specs=(P(), P(("sect", "tok"), "vocab"), P(("tok", "vocab"), "sect")),
        check_vma=False,
    )
```

```python
import functools

import jax
import jax.numpy as jnp
from jax import lax
from jax.experimental import pallas as pl
from jax.experimental.pallas import tpu as pltpu
from jax.sharding import PartitionSpec as P


def softened(teacher_logits, student_logits):
    teacher = teacher_logits * 0.5
    student = student_logits * 0.5
    teacher_exp = jnp.exp(teacher)
    student_exp = jnp.exp(student)
    partial_sums = (
        jnp.sum(teacher_exp, axis=1),
        jnp.sum(student_exp, axis=1),
        jnp.sum(teacher_exp * (teacher - student), axis=1),
    )
    return (teacher_exp, student_exp, partial_sums)


def finish(teacher_exp, student_exp, totals, live_rows, live_total, vocab_entries):
    teacher_sum, student_sum, cross = totals
    divergence = cross / teacher_sum - jnp.log(teacher_sum) + jnp.log(student_sum)
    numerator = jnp.sum(live_rows * divergence)
    row_scale = live_rows * (32.0 * vocab_entries * 0.5 / live_total)
    logit_grad = (
        row_scale[:, None]
        * (student_exp / student_sum[:, None] - teacher_exp / teacher_sum[:, None])
    ).astype(jnp.bfloat16)
    return (logit_grad, numerator)


def body(teacher_hidden, teacher_head, student_hidden, student_head, live_counts):
    token_rows = teacher_hidden.shape[0]
    vocab_entries = student_head.shape[1] * lax.axis_size("vocab")
    live_total = lax.psum(jnp.sum(live_counts.astype(jnp.float32)), "tok")
    live_rows = (jnp.arange(token_rows, dtype=jnp.int32) < live_counts[0]).astype(jnp.float32)
    teacher_part = jnp.dot(teacher_hidden, teacher_head, preferred_element_type=jnp.float32)
    student_part = jnp.dot(student_hidden, student_head, preferred_element_type=jnp.float32)
    teacher_logits, student_logits = lax.psum((teacher_part, student_part), "sect")
    teacher_exp, student_exp, partial_sums = softened(teacher_logits, student_logits)
    totals = lax.psum((partial_sums[0], partial_sums[1], partial_sums[2]), "vocab")
    logit_grad, numerator = finish(
        teacher_exp, student_exp, totals, live_rows, live_total, vocab_entries
    )
    owned_features = lax.all_to_all(student_hidden, "tok", split_axis=1, concat_axis=0, tiled=True)
    head_sum = lax.dot_general(
        owned_features,
        lax.all_gather(logit_grad, "tok", axis=0, tiled=True),
        (((0,), (0,)), ((), ())),
        preferred_element_type=jnp.float32,
    )
    head_grad = head_sum.astype(jnp.bfloat16)
    hidden_grad = lax.psum_scatter(
        lax.dot_general(
            logit_grad, student_head, (((1,), (1,)), ((), ())), preferred_element_type=jnp.float32
        ),
        "vocab",
        scatter_dimension=0,
        tiled=True,
    ).astype(jnp.bfloat16)
    loss = lax.psum(numerator, "tok") / live_total
    return (loss, head_grad, hidden_grad)


MESH = pl.DeviceIdType.MESH
TILE = 32
F32, BF16 = jnp.float32, jnp.bfloat16


def fused(
    n_tok, n_in, n_out, kc, plans,
    counts, th_hbm, thead_hbm, sh_hbm, shead_hbm,
    loss_ref, head_ref, hid_ref,
    th, thead, sh, shead, turned, spart, tpart, srecv, trecv, slog, te_ref, se_ref, stat, ssend, zrecv,
    cnt, crecv, num, nrecv, hown, hrecv, grad, grecv, head_acc,
    coef, apart, pre_b, pre_r, zt_f, zt_b, zt_r, zs_f, zs_b, zs_r, yt_f, yt_b, yt_r, ys_f, ys_b, ys_r,
    load_sem, p_ss, p_rs, c_ss, c_rs, h_ss, h_rs, s_ss, s_rs, g_ss, g_rs, n_ss, n_rs,
    o_ss, o_rs, za_ss, za_rs, zb_ss, zb_rs, ya_ss, ya_rs, yb_ss, yb_rs, pre_ss, pre_rs,
):
    sect, tok, voc = lax.axis_index("sect"), lax.axis_index("tok"), lax.axis_index("vocab")
    _, n_voc, sub, feats = sh.shape
    half, rows, width = n_voc * sub, 2 * n_voc * sub, shead.shape[1]
    steps = th.shape[0]
    inner, outer = voc % n_in, voc // n_in
    across, oth = 1 - inner, 1 - sect
    out_peers = [(outer + d) % n_out for d in range(1, n_out)]
    block = feats // n_tok
    other = {"sect": oth}
    tok_peers = [(tok + d) % n_tok for d in range(1, n_tok)]
    voc_peers = [(voc + d) % n_voc for d in range(1, n_voc)]
    sum_peers = [(s, (tok + d) % n_tok) for d in range(n_tok) for s in (sect, oth)][1:]

    sh_loads = [pltpu.make_async_copy(sh_hbm.at[:, q], sh.at[q], load_sem.at[q]) for q in (0, 1)]
    sh_loads.append(pltpu.make_async_copy(shead_hbm, shead, load_sem.at[2]))
    th_loads = [
        [
            pltpu.make_async_copy(
                th_hbm.at[:, q, :, pl.ds(k * kc, kc)], th.at[k, q], load_sem.at[3 + 3 * k + q]
            )
            for q in (0, 1)
        ]
        + [
            pltpu.make_async_copy(
                thead_hbm.at[pl.ds(k * kc, kc)], thead.at[k], load_sem.at[5 + 3 * k]
            )
        ]
        for k in range(steps)
    ]
    for load in sh_loads + sum(th_loads, []):
        load.start()
    barrier = pltpu.get_barrier_semaphore()
    for s, p in sum_peers:
        pl.semaphore_signal(
            barrier, inc=1, device_id={"sect": s, "tok": p}, device_id_type=MESH
        )
    for p in voc_peers:
        pl.semaphore_signal(barrier, inc=1, device_id={"vocab": p}, device_id_type=MESH)


    def make(src, dst, ss, rs, to):
        return pltpu.make_async_remote_copy(
            src_ref=src, dst_ref=dst, send_sem=ss, recv_sem=rs, device_id=to, device_id_type=MESH
        )

    def send(*args):
        copy = make(*args)
        copy.start()
        return copy

    cnt[...] = jnp.full(cnt.shape, counts[0].astype(F32))
    for load in sh_loads:
        load.wait()
    spart[...] = jnp.dot(
        sh[...].reshape(rows, feats), shead[...], preferred_element_type=F32
    ).reshape(2, half, width)
    pl.semaphore_wait(barrier, len(sum_peers) + n_voc - 1)
    c_cp, h_cp, s_cp = [], [], []
    p_cp = [send(spart.at[oth], srecv, p_ss.at[0], p_rs.at[0], other)]
    for i, p in enumerate(tok_peers):
        c_cp.append(send(cnt, crecv.at[i], c_ss.at[i], c_rs.at[i], {"tok": p}))
        cols = pl.ds(pl.multiple_of(p * block, block), block)
        h_cp.append(
            send(sh.at[:, :, :, cols], hrecv.at[i], h_ss.at[i], h_rs.at[i], {"tok": p})
        )
    for k in range(steps):
        for load in th_loads[k]:
            load.wait()
        if k < steps - 1:
            term = jnp.dot(
                th[k].reshape(rows, kc), thead[k], preferred_element_type=F32
            ).reshape(2, half, width)
            tpart[...] = term if k == 0 else tpart[...] + term
            continue
        for q in (oth, sect):
            tpart[q] = tpart[q] + jnp.dot(
                th[k, q].reshape(half, kc), thead[k], preferred_element_type=F32
            )
            if q is oth:
                p_cp.append(send(tpart.at[oth], trecv, p_ss.at[1], p_rs.at[1], other))
    def soften_student(i, carry):
        at = pl.ds(pl.multiple_of(i * TILE, TILE), TILE)
        s = (spart[sect, at, :] + srecv[at, :]) * 0.5
        slog[at, :] = s
        se_ref[at, :] = jnp.exp(s)
        return carry

    p_cp[0].wait_recv()
    lax.fori_loop(0, half // TILE, soften_student, 0, unroll=True)
    p_cp[1].wait_recv()

    lane = lax.broadcasted_iota(jnp.int32, (TILE, 128), 1)

    def soften(i, carry):
        at = pl.ds(pl.multiple_of(i * TILE, TILE), TILE)
        s = slog[at, :]
        t = (tpart[sect, at, :] + trecv[at, :]) * 0.5
        te, se = jnp.exp(t), se_ref[at, :]
        te_ref[at, :] = te
        zt = jnp.sum(te, axis=1, keepdims=True)
        zs = jnp.sum(se, axis=1, keepdims=True)
        cross = jnp.sum(te * (t - s), axis=1, keepdims=True)
        stat[at, :] = jnp.where(lane == 0, zt, jnp.where(lane == 1, zs, cross))
        return carry

    lax.fori_loop(0, half // TILE, soften, 0, unroll=True)
    ssend[...] = stat[...].T[:4]
    for i, p in enumerate(voc_peers):
        s_cp.append(send(ssend, zrecv.at[i], s_ss.at[i], s_rs.at[i], {"vocab": p}))

    def ahead(fa, f):
        w = fa[f]
        return make(
            pre_b.at[f, :, :, :, 0:w], pre_r.at[f, :, :, :, 0:w], pre_ss.at[f], pre_rs.at[f],
            {"vocab": outer * n_in + across},
        )

    def early(fz, fa, n_pre, late):
        if not n_pre:
            return
        for z in range(n_out):
            at = pl.ds(pl.multiple_of((z * n_in + across) * sub, sub), sub)
            zt, zs = stat[at, 0:1], stat[at, 1:2]
            t = te_ref[at, :] * jnp.where(zt > 0, 1.0 / zt, 0.0)
            s = se_ref[at, :] * jnp.where(zs > 0, 1.0 / zs, 0.0)
            apart[0, z] = (s - t).astype(BF16)
            apart[1, z] = t.astype(BF16)
        start = fz
        for f in range(n_pre):
            w = fa[f]
            pre_b[f, :, :, :, 0:w] = jnp.dot(
                apart[...].reshape(2 * n_out * sub, width), turned[:, start:start + w],
                preferred_element_type=F32,
            ).reshape(2, n_out, sub, w).astype(BF16)
            ahead(fa, f).start()
            start += w

    mine_cols = pl.ds(pl.multiple_of(tok * block, block), block)
    turned[...] = shead[...].T
    for core, plan in enumerate(plans):
        pl.when(sect == core)(functools.partial(early, *plan))
    hown[...] = sh[:, :, :, mine_cols].reshape(rows, block).T
    for copy in c_cp:
        copy.wait_recv()
    total = cnt[...]
    for i in range(n_tok - 1):
        total = total + crecv[i]
    live_total = total[0:1, 0:1]
    scale = 32.0 * (width * n_voc) * 0.5 / live_total
    place = lax.broadcasted_iota(jnp.int32, (1, half), 1)
    row = (place // sub) * (2 * sub) + sect * sub + place % sub
    live = (row.astype(F32) < cnt[0:1, 0:1]).astype(F32)
    totals = ssend[...]
    for i, copy in enumerate(s_cp):
        copy.wait_recv()
        totals = totals + zrecv[i]
    zt, zs, cross = totals[0:1], totals[1:2], totals[2:3]
    a, b = live * scale / zs, live * scale / zt
    slot = (voc - (outer * n_in + across) + n_voc) % n_voc - 1
    peer = zrecv[slot]
    ahead_s = a * peer[1:2]
    scales = jnp.concatenate([a, b, ahead_s, ahead_s - b * peer[0:1]] * 2, axis=0)
    coef[...] = jnp.concatenate([scales] * 16, axis=0).T.reshape(n_out, n_in, sub, 128)

    def finish_tile(i, carry):
        at = pl.ds(pl.multiple_of(i * n_in * sub, n_in * sub), n_in * sub)
        c = coef[i].reshape(n_in * sub, 128)
        g = c[:, 0:1] * se_ref[at, :] - c[:, 1:2] * te_ref[at, :]
        grad[sect, i] = g.reshape(n_in, sub, width).astype(BF16)
        return carry

    lax.fori_loop(0, n_out, finish_tile, 0, unroll=True)
    o_cp = send(grad.at[sect], grad.at[sect], o_ss, o_rs, other)

    def spread(fz, fa, n_pre, late):
        zb_cp, yb_cp = {}, {}
        starts = [fz + sum(fa[:f]) for f in range(len(fa))]
        pair, zp = {"vocab": outer * n_in + across}, [{"vocab": p * n_in + inner} for p in out_peers]
        za_cp = {
            (j, i): make(zt_b.at[j, p, :, :, 0:fz], zt_r.at[j, i, :, :, 0:fz],
                         za_ss.at[j, i], za_rs.at[j, i], zp[i])
            for j in range(2) for i, p in enumerate(out_peers) if fz
        }
        ya_cp = {
            (j, f): make(yt_b.at[j, f, :, across, :, 0:w], yt_r.at[j, f, :, :, 0:w],
                         ya_ss.at[j, f], ya_rs.at[j, f], pair)
            for j in range(2) for f, w in enumerate(fa) if j or f >= n_pre
        }

        def product(g, start, size):
            return jnp.dot(
                g, turned[:, start:start + size], preferred_element_type=F32
            ).reshape(n_out, n_in, sub, size)

        def z_terms(j, g):
            term = product(g, 0, fz)
            zt_f[j, :, :, :, 0:fz] = term
            zt_b[j, :, :, :, 0:fz] = term.astype(BF16)
            for i in range(n_out - 1):
                za_cp[j, i].start()

        def y_terms(j, g):
            for f, w in enumerate(fa):
                if j == 0 and f < n_pre:
                    continue
                term = product(g, starts[f], w)
                yt_f[j, f, :, :, :, 0:w] = term
                yt_b[j, f, :, :, :, 0:w] = term.astype(BF16)
                ya_cp[j, f].start()

        def terms(j, q):
            g = grad[q].reshape(half, width)
            if fz:
                z_terms(j, g)
            if not late:
                y_terms(j, g)
            for i, p in enumerate(tok_peers):
                g_cp.append(
                    send(grad.at[q], grecv.at[i, q], g_ss.at[i, j], g_rs.at[i, j], {"tok": p})
                )

        def take_z(j):
            part = zt_f[j, outer, :, :, 0:fz]
            for i in range(n_out - 1):
                za_cp[j, i].wait_recv()
                part = part + zt_r[j, i, :, :, 0:fz].astype(F32)
            zs_f[j, :, :, 0:fz] = part
            zs_b[j, :, :, 0:fz] = part.astype(BF16)
            yb_cp[j] = send(
                zs_b.at[j, across, :, 0:fz], zs_r.at[j, :, 0:fz], yb_ss.at[j], yb_rs.at[j], pair
            )

        def take_pre(f):
            w = fa[f]
            ahead(fa, f).wait_recv()
            g = grad[sect, :, inner].reshape(n_out * sub, width)
            own = jnp.dot(
                g, turned[:, starts[f]:starts[f] + w], preferred_element_type=F32
            ).reshape(n_out, sub, w)
            c = coef[:, inner]
            both = (
                own
                + c[:, :, 2:3] * pre_r[f, 0, :, :, 0:w].astype(F32)
                + c[:, :, 3:4] * pre_r[f, 1, :, :, 0:w].astype(F32)
            )
            pass_on(0, f, both)

        def take_y(j, f):
            w = fa[f]
            ya_cp[j, f].wait_recv()
            pass_on(j, f, yt_f[j, f, :, inner, :, 0:w] + yt_r[j, f, :, :, 0:w].astype(F32))

        def pass_on(j, f, both):
            w = fa[f]
            ys_f[j, f, :, :, 0:w] = both
            ys_b[j, f, :, :, 0:w] = both.astype(BF16)
            for i, p in enumerate(out_peers):
                zb_cp[j, f, i] = send(
                    ys_b.at[j, f, p, :, 0:w], ys_r.at[j, f, i, :, 0:w],
                    zb_ss.at[j, f, i], zb_rs.at[j, f, i], zp[i],
                )

        g_cp, n_cp = [], []
        terms(0, sect)
        o_cp.wait_recv()
        terms(1, oth)
        for f in range(n_pre):
            take_pre(f)
        kl = cross / zt - jnp.log(zt) + jnp.log(zs)
        num[...] = jnp.broadcast_to(jnp.sum(live * kl, axis=1, keepdims=True), num.shape)
        for i, (s, p) in enumerate(sum_peers):
            n_cp.append(send(num, nrecv.at[i], n_ss.at[i], n_rs.at[i], {"sect": s, "tok": p}))
        head_acc[...] = jnp.dot(
            hown[...], grad[...].reshape(rows, width), preferred_element_type=F32
        )
        if late:
            take_z(0)
            y_terms(0, grad[sect].reshape(half, width))
            y_terms(1, grad[oth].reshape(half, width))
            take_z(1)
        for j in range(2):
            for f in range(len(fa)):
                if j or f >= n_pre:
                    take_y(j, f)
                if fz and f == 0 and not late:
                    take_z(j)

        head = head_acc[...]
        numerator = num[...]
        for i, copy in enumerate(n_cp):
            copy.wait_recv()
            numerator = numerator + nrecv[i]
        for i in range(n_tok - 1):
            h_cp[i].wait_recv()
            theirs = hrecv[i].reshape(rows, block).T
            g_cp[i].wait_recv()
            g_cp[n_tok - 1 + i].wait_recv()
            head = head + jnp.dot(
                theirs, grecv[i].reshape(rows, width), preferred_element_type=F32
            )
        head_ref[...] = head.astype(BF16)
        loss_ref[...] = numerator / live_total

        for j, q in ((0, sect), (1, oth)):
            if fz:
                yb_cp[j].wait_recv()
                mine = zs_f[j, inner, :, 0:fz] + zs_r[j, :, 0:fz].astype(F32)
                hid_ref[q, :, 0:fz] = mine.astype(BF16)
            for f, w in enumerate(fa):
                hid = ys_f[j, f, outer, :, 0:w]
                for i in range(n_out - 1):
                    zb_cp[j, f, i].wait_recv()
                    hid = hid + ys_r[j, f, i, :, 0:w].astype(F32)
                hid_ref[q, :, starts[f]:starts[f] + w] = hid.astype(BF16)
        for copy in g_cp + n_cp:
            copy.wait_send()
        for f in range(n_pre):
            ahead(fa, f).wait_send()
        for group in (za_cp, zb_cp, ya_cp, yb_cp):
            for copy in group.values():
                copy.wait_send()

    for core, plan in enumerate(plans):
        pl.when(sect == core)(functools.partial(spread, *plan))
    o_cp.wait_send()
    for copy in p_cp + c_cp + h_cp + s_cp:
        copy.wait_send()


def emit(loss_in, head_in, hid_in, loss_out, head_out, hid_out, sems):
    copies = [
        pltpu.make_async_copy(head_in, head_out, sems.at[0]),
        pltpu.make_async_copy(hid_in, hid_out, sems.at[1]),
    ]
    for copy in copies:
        copy.start()
    loss_out[...] = loss_in[0:1, 0:1]
    for copy in copies:
        copy.wait()


def fused_body(n_tok, n_voc, teacher_hidden, teacher_head, student_hidden, student_head, live_counts):
    rows, t_feats = teacher_hidden.shape
    feats, width = student_head.shape
    kc = t_feats // 4
    third, fourth = feats // 3, feats // 4
    plans = (
        (0, (third,) * 3, 2, False),
        (third, (fourth, feats - third - fourth), 1, True),
    )
    fz = max(plan[0] for plan in plans)
    fw = max(max(plan[1]) for plan in plans)
    ny = max(len(plan[1]) for plan in plans)
    block, out_rows, half = feats // n_tok, rows // n_voc, rows // 2
    sub = out_rows // 2
    n_in, n_out = 2, n_voc // 2
    tp, vp, op, sp = n_tok - 1, n_voc - 1, n_out - 1, 2 * n_tok - 1
    steps = t_feats // kc
    vmem, dma = pltpu.VMEM, pltpu.SemaphoreType.DMA
    any_spec = pl.BlockSpec(memory_space=pl.ANY)
    vm_spec = pl.BlockSpec(memory_space=pltpu.VMEM)
    loss, head, hid = pl.pallas_call(
        functools.partial(fused, n_tok, n_in, n_out, kc, plans),
        out_shape=(
            jax.ShapeDtypeStruct((8, 128), F32),
            jax.ShapeDtypeStruct((block, width), BF16),
            jax.ShapeDtypeStruct((2, sub, feats), BF16),
        ),
        in_specs=[pl.BlockSpec(memory_space=pltpu.SMEM)] + [any_spec] * 4,
        out_specs=(vm_spec,) * 3,
        scratch_shapes=[
            vmem((steps, 2, n_voc, sub, kc), BF16), vmem((steps, kc, width), BF16),
            vmem((2, n_voc, sub, feats), BF16), vmem((feats, width), BF16), vmem((width, feats), BF16),
            vmem((2, half, width), F32), vmem((2, half, width), F32),
            vmem((half, width), F32), vmem((half, width), F32), vmem((half, width), F32),
            vmem((half, width), F32), vmem((half, width), F32),
            vmem((half, 128), F32), vmem((4, half), F32), vmem((vp, 4, half), F32),
            vmem((8, 128), F32), vmem((tp, 8, 128), F32),
            vmem((8, 128), F32), vmem((sp, 8, 128), F32),
            vmem((block, rows), BF16), vmem((tp, 2, n_voc, sub, block), BF16),
            vmem((2, n_out, n_in, sub, width), BF16), vmem((tp, 2, n_out, n_in, sub, width), BF16),
            vmem((block, width), F32),
            vmem((n_out, n_in, sub, 128), F32), vmem((2, n_out, sub, width), BF16),
            vmem((ny, 2, n_out, sub, fw), BF16), vmem((ny, 2, n_out, sub, fw), BF16),
            vmem((2, n_out, n_in, sub, fz), F32), vmem((2, n_out, n_in, sub, fz), BF16),
            vmem((2, op, n_in, sub, fz), BF16),
            vmem((2, n_in, sub, fz), F32), vmem((2, n_in, sub, fz), BF16),
            vmem((2, sub, fz), BF16),
            vmem((2, ny, n_out, n_in, sub, fw), F32), vmem((2, ny, n_out, n_in, sub, fw), BF16),
            vmem((2, ny, n_out, sub, fw), BF16),
            vmem((2, ny, n_out, sub, fw), F32), vmem((2, ny, n_out, sub, fw), BF16),
            vmem((2, ny, op, sub, fw), BF16),
            dma((3 + 3 * steps,)), dma((2,)), dma((2,)), dma((tp,)), dma((tp,)), dma((tp,)), dma((tp,)),
            dma((vp,)), dma((vp,)), dma((tp, 2)), dma((tp, 2)), dma((sp,)), dma((sp,)),
            dma(()), dma(()), dma((2, op)), dma((2, op)), dma((2, ny, op)), dma((2, ny, op)),
            dma((2, ny)), dma((2, ny)), dma((2,)), dma((2,)), dma((ny,)), dma((ny,)),
        ],
        compiler_params=pltpu.CompilerParams(
            collective_id=0, has_side_effects=True, vmem_limit_bytes=53 * 1024 * 1024
        ),
    )(
        live_counts, teacher_hidden.reshape(n_voc, 2, sub, t_feats), teacher_head,
        student_hidden.reshape(n_voc, 2, sub, feats), student_head,
    )
    hid = hid.reshape(out_rows, feats)
    loss, head, hid = pl.pallas_call(
        emit,
        out_shape=(
            jax.ShapeDtypeStruct((1, 1), F32),
            jax.ShapeDtypeStruct(head.shape, BF16),
            jax.ShapeDtypeStruct(hid.shape, BF16),
        ),
        in_specs=[vm_spec, any_spec, any_spec],
        out_specs=(vm_spec, any_spec, any_spec),
        scratch_shapes=[dma((2,))],
        compiler_params=pltpu.CompilerParams(vmem_limit_bytes=4 * 1024 * 1024),
    )(loss, head, hid)
    return (loss[0, 0], head, hid)


def solution(mesh):
    placed = (P("tok", "sect"), P("sect", "vocab"), P("tok", "sect"), P("sect", "vocab"), P("tok"))
    n_tok, n_voc = mesh.shape["tok"], mesh.shape["vocab"]

    def run(*args):
        rows = args[0].shape[0]
        fits = rows == 256 and rows % (TILE * n_voc) == 0 and n_voc % 2 == 0 and n_voc > 2
        fits = fits and args[2].shape[1] % (12 * 128) == 0 and args[2].shape[1] % (128 * n_tok) == 0
        if fits and n_tok > 1:
            return fused_body(n_tok, n_voc, *args)
        return body(*args)

    return jax.shard_map(
        run,
        mesh=mesh,
        in_specs=placed,
        out_specs=(P(), P(("sect", "tok"), "vocab"), P(("tok", "vocab"), "sect")),
        check_vma=False,
    )
```

```python
import functools

import jax
import jax.numpy as jnp
from jax import lax
from jax.experimental import pallas as pl
from jax.experimental.pallas import tpu as pltpu
from jax.sharding import PartitionSpec as P


def softened(teacher_logits, student_logits):
    teacher = teacher_logits * 0.5
    student = student_logits * 0.5
    teacher_exp = jnp.exp(teacher)
    student_exp = jnp.exp(student)
    partial_sums = (
        jnp.sum(teacher_exp, axis=1),
        jnp.sum(student_exp, axis=1),
        jnp.sum(teacher_exp * (teacher - student), axis=1),
    )
    return (teacher_exp, student_exp, partial_sums)


def finish(teacher_exp, student_exp, totals, live_rows, live_total, vocab_entries):
    teacher_sum, student_sum, cross = totals
    divergence = cross / teacher_sum - jnp.log(teacher_sum) + jnp.log(student_sum)
    numerator = jnp.sum(live_rows * divergence)
    row_scale = live_rows * (32.0 * vocab_entries * 0.5 / live_total)
    logit_grad = (
        row_scale[:, None]
        * (student_exp / student_sum[:, None] - teacher_exp / teacher_sum[:, None])
    ).astype(jnp.bfloat16)
    return (logit_grad, numerator)


def body(teacher_hidden, teacher_head, student_hidden, student_head, live_counts):
    token_rows = teacher_hidden.shape[0]
    vocab_entries = student_head.shape[1] * lax.axis_size("vocab")
    live_total = lax.psum(jnp.sum(live_counts.astype(jnp.float32)), "tok")
    live_rows = (jnp.arange(token_rows, dtype=jnp.int32) < live_counts[0]).astype(jnp.float32)
    teacher_part = jnp.dot(teacher_hidden, teacher_head, preferred_element_type=jnp.float32)
    student_part = jnp.dot(student_hidden, student_head, preferred_element_type=jnp.float32)
    teacher_logits, student_logits = lax.psum((teacher_part, student_part), "sect")
    teacher_exp, student_exp, partial_sums = softened(teacher_logits, student_logits)
    totals = lax.psum((partial_sums[0], partial_sums[1], partial_sums[2]), "vocab")
    logit_grad, numerator = finish(
        teacher_exp, student_exp, totals, live_rows, live_total, vocab_entries
    )
    owned_features = lax.all_to_all(student_hidden, "tok", split_axis=1, concat_axis=0, tiled=True)
    head_sum = lax.dot_general(
        owned_features,
        lax.all_gather(logit_grad, "tok", axis=0, tiled=True),
        (((0,), (0,)), ((), ())),
        preferred_element_type=jnp.float32,
    )
    head_grad = head_sum.astype(jnp.bfloat16)
    hidden_grad = lax.psum_scatter(
        lax.dot_general(
            logit_grad, student_head, (((1,), (1,)), ((), ())), preferred_element_type=jnp.float32
        ),
        "vocab",
        scatter_dimension=0,
        tiled=True,
    ).astype(jnp.bfloat16)
    loss = lax.psum(numerator, "tok") / live_total
    return (loss, head_grad, hidden_grad)


MESH = pl.DeviceIdType.MESH
TILE = 32
F32, BF16 = jnp.float32, jnp.bfloat16


def fused(
    n_tok, n_in, n_out, kc, plans,
    counts, th_hbm, thead_hbm, sh_hbm, shead_hbm,
    loss_ref, head_ref, hid_ref,
    th, thead, sh, shead, turned, spart, tpart, srecv, trecv, slog, te_ref, se_ref, stat, ssend, zrecv,
    cnt, crecv, num, nrecv, hown, hrecv, grad, grecv, head_acc,
    coef, apart, pre_b, pre_r, zt_f, zt_b, zt_r, zs_f, zs_b, zs_r, yt_f, yt_b, yt_r, ys_f, ys_b, ys_r,
    load_sem, p_ss, p_rs, c_ss, c_rs, h_ss, h_rs, s_ss, s_rs, g_ss, g_rs, n_ss, n_rs,
    o_ss, o_rs, za_ss, za_rs, zb_ss, zb_rs, ya_ss, ya_rs, yb_ss, yb_rs, pre_ss, pre_rs,
):
    sect, tok, voc = lax.axis_index("sect"), lax.axis_index("tok"), lax.axis_index("vocab")
    _, n_voc, sub, feats = sh.shape
    half, rows, width = n_voc * sub, 2 * n_voc * sub, shead.shape[1]
    steps = th.shape[0]
    inner, outer = voc % n_in, voc // n_in
    across, oth = 1 - inner, 1 - sect
    out_peers = [(outer + d) % n_out for d in range(1, n_out)]
    block = feats // n_tok
    other = {"sect": oth}
    tok_peers = [(tok + d) % n_tok for d in range(1, n_tok)]
    voc_peers = [(voc + d) % n_voc for d in range(1, n_voc)]
    sum_peers = [(s, (tok + d) % n_tok) for d in range(n_tok) for s in (sect, oth)][1:]

    sh_loads = [pltpu.make_async_copy(sh_hbm.at[:, q], sh.at[q], load_sem.at[q]) for q in (0, 1)]
    sh_loads.append(pltpu.make_async_copy(shead_hbm, shead, load_sem.at[2]))
    th_loads = [
        [
            pltpu.make_async_copy(
                th_hbm.at[:, q, :, pl.ds(k * kc, kc)], th.at[k, q], load_sem.at[3 + 3 * k + q]
            )
            for q in (0, 1)
        ]
        + [
            pltpu.make_async_copy(
                thead_hbm.at[pl.ds(k * kc, kc)], thead.at[k], load_sem.at[5 + 3 * k]
            )
        ]
        for k in range(steps)
    ]
    for load in sh_loads + sum(th_loads, []):
        load.start()
    barrier = pltpu.get_barrier_semaphore()
    for s, p in sum_peers:
        pl.semaphore_signal(
            barrier, inc=1, device_id={"sect": s, "tok": p}, device_id_type=MESH
        )
    for p in voc_peers:
        pl.semaphore_signal(barrier, inc=1, device_id={"vocab": p}, device_id_type=MESH)


    def make(src, dst, ss, rs, to):
        return pltpu.make_async_remote_copy(
            src_ref=src, dst_ref=dst, send_sem=ss, recv_sem=rs, device_id=to, device_id_type=MESH
        )

    def send(*args):
        copy = make(*args)
        copy.start()
        return copy

    cnt[...] = jnp.full(cnt.shape, counts[0].astype(F32))
    for load in sh_loads:
        load.wait()
    spart[...] = jnp.dot(
        sh[...].reshape(rows, feats), shead[...], preferred_element_type=F32
    ).reshape(2, half, width)
    pl.semaphore_wait(barrier, len(sum_peers) + n_voc - 1)
    c_cp, h_cp, s_cp = [], [], []
    p_cp = [send(spart.at[oth], srecv, p_ss.at[0], p_rs.at[0], other)]
    for i, p in enumerate(tok_peers):
        c_cp.append(send(cnt, crecv.at[i], c_ss.at[i], c_rs.at[i], {"tok": p}))
        cols = pl.ds(pl.multiple_of(p * block, block), block)
        h_cp.append(
            send(sh.at[:, :, :, cols], hrecv.at[i], h_ss.at[i], h_rs.at[i], {"tok": p})
        )
    for k in range(steps):
        for load in th_loads[k]:
            load.wait()
        if k < steps - 1:
            term = jnp.dot(
                th[k].reshape(rows, kc), thead[k], preferred_element_type=F32
            ).reshape(2, half, width)
            tpart[...] = term if k == 0 else tpart[...] + term
            continue
        for n in range(2):
            lo, hi = n * width // 2, (n + 1) * width // 2
            tpart[oth, :, lo:hi] = tpart[oth, :, lo:hi] + jnp.dot(
                th[k, oth].reshape(half, kc), thead[k, :, lo:hi], preferred_element_type=F32
            )
            p_cp.append(
                send(tpart.at[oth, :, lo:hi], trecv.at[:, lo:hi],
                     p_ss.at[1 + n], p_rs.at[1 + n], other)
            )
        tpart[sect] = tpart[sect] + jnp.dot(
            th[k, sect].reshape(half, kc), thead[k], preferred_element_type=F32
        )
    def soften_student(i, carry):
        at = pl.ds(pl.multiple_of(i * TILE, TILE), TILE)
        s = (spart[sect, at, :] + srecv[at, :]) * 0.5
        slog[at, :] = s
        se_ref[at, :] = jnp.exp(s)
        return carry

    p_cp[0].wait_recv()
    lax.fori_loop(0, half // TILE, soften_student, 0, unroll=True)
    for copy in p_cp[1:]:
        copy.wait_recv()

    lane = lax.broadcasted_iota(jnp.int32, (TILE, 128), 1)

    def soften(i, carry):
        at = pl.ds(pl.multiple_of(i * TILE, TILE), TILE)
        s = slog[at, :]
        t = (tpart[sect, at, :] + trecv[at, :]) * 0.5
        te, se = jnp.exp(t), se_ref[at, :]
        te_ref[at, :] = te
        zt = jnp.sum(te, axis=1, keepdims=True)
        zs = jnp.sum(se, axis=1, keepdims=True)
        cross = jnp.sum(te * (t - s), axis=1, keepdims=True)
        stat[at, :] = jnp.where(lane == 0, zt, jnp.where(lane == 1, zs, cross))
        return carry

    lax.fori_loop(0, half // TILE, soften, 0, unroll=True)
    ssend[...] = stat[...].T[:4]
    for i, p in enumerate(voc_peers):
        s_cp.append(send(ssend, zrecv.at[i], s_ss.at[i], s_rs.at[i], {"vocab": p}))

    def ahead(fa, f):
        w = fa[f]
        return make(
            pre_b.at[f, :, :, :, 0:w], pre_r.at[f, :, :, :, 0:w], pre_ss.at[f], pre_rs.at[f],
            {"vocab": outer * n_in + across},
        )

    def early(fz, fa, n_pre, late):
        if not n_pre:
            return
        for z in range(n_out):
            at = pl.ds(pl.multiple_of((z * n_in + across) * sub, sub), sub)
            zt, zs = stat[at, 0:1], stat[at, 1:2]
            t = te_ref[at, :] * jnp.where(zt > 0, 1.0 / zt, 0.0)
            s = se_ref[at, :] * jnp.where(zs > 0, 1.0 / zs, 0.0)
            apart[0, z] = (s - t).astype(BF16)
            apart[1, z] = t.astype(BF16)
        start = fz
        for f in range(n_pre):
            w = fa[f]
            pre_b[f, :, :, :, 0:w] = jnp.dot(
                apart[...].reshape(2 * n_out * sub, width), turned[:, start:start + w],
                preferred_element_type=F32,
            ).reshape(2, n_out, sub, w).astype(BF16)
            ahead(fa, f).start()
            start += w

    mine_cols = pl.ds(pl.multiple_of(tok * block, block), block)
    turned[...] = shead[...].T
    for core, plan in enumerate(plans):
        pl.when(sect == core)(functools.partial(early, *plan))
    hown[...] = sh[:, :, :, mine_cols].reshape(rows, block).T
    for copy in c_cp:
        copy.wait_recv()
    total = cnt[...]
    for i in range(n_tok - 1):
        total = total + crecv[i]
    live_total = total[0:1, 0:1]
    scale = 32.0 * (width * n_voc) * 0.5 / live_total
    place = lax.broadcasted_iota(jnp.int32, (1, half), 1)
    row = (place // sub) * (2 * sub) + sect * sub + place % sub
    live = (row.astype(F32) < cnt[0:1, 0:1]).astype(F32)
    totals = ssend[...]
    for i, copy in enumerate(s_cp):
        copy.wait_recv()
        totals = totals + zrecv[i]
    zt, zs, cross = totals[0:1], totals[1:2], totals[2:3]
    a, b = live * scale / zs, live * scale / zt
    slot = (voc - (outer * n_in + across) + n_voc) % n_voc - 1
    peer = zrecv[slot]
    ahead_s = a * peer[1:2]
    scales = jnp.concatenate([a, b, ahead_s, ahead_s - b * peer[0:1]] * 2, axis=0)
    coef[...] = jnp.concatenate([scales] * 16, axis=0).T.reshape(n_out, n_in, sub, 128)

    def finish_tile(i, carry):
        at = pl.ds(pl.multiple_of(i * n_in * sub, n_in * sub), n_in * sub)
        c = coef[i].reshape(n_in * sub, 128)
        g = c[:, 0:1] * se_ref[at, :] - c[:, 1:2] * te_ref[at, :]
        grad[sect, i] = g.reshape(n_in, sub, width).astype(BF16)
        return carry

    lax.fori_loop(0, n_out, finish_tile, 0, unroll=True)
    o_cp = send(grad.at[sect], grad.at[sect], o_ss, o_rs, other)

    def spread(fz, fa, n_pre, late):
        zb_cp, yb_cp = {}, {}
        starts = [fz + sum(fa[:f]) for f in range(len(fa))]
        pair, zp = {"vocab": outer * n_in + across}, [{"vocab": p * n_in + inner} for p in out_peers]
        za_cp = {
            (j, i): make(zt_b.at[j, p, :, :, 0:fz], zt_r.at[j, i, :, :, 0:fz],
                         za_ss.at[j, i], za_rs.at[j, i], zp[i])
            for j in range(2) for i, p in enumerate(out_peers) if fz
        }
        ya_cp = {
            (j, f): make(yt_b.at[j, f, :, across, :, 0:w], yt_r.at[j, f, :, :, 0:w],
                         ya_ss.at[j, f], ya_rs.at[j, f], pair)
            for j in range(2) for f, w in enumerate(fa) if j or f >= n_pre
        }

        def product(g, start, size):
            return jnp.dot(
                g, turned[:, start:start + size], preferred_element_type=F32
            ).reshape(n_out, n_in, sub, size)

        def z_terms(j, g):
            term = product(g, 0, fz)
            zt_f[j, :, :, :, 0:fz] = term
            zt_b[j, :, :, :, 0:fz] = term.astype(BF16)
            for i in range(n_out - 1):
                za_cp[j, i].start()

        def y_terms(j, g):
            for f, w in enumerate(fa):
                if j == 0 and f < n_pre:
                    continue
                term = product(g, starts[f], w)
                yt_f[j, f, :, :, :, 0:w] = term
                yt_b[j, f, :, :, :, 0:w] = term.astype(BF16)
                ya_cp[j, f].start()

        def terms(j, q):
            g = grad[q].reshape(half, width)
            if fz:
                z_terms(j, g)
            if not late:
                y_terms(j, g)
            for i, p in enumerate(tok_peers):
                g_cp.append(
                    send(grad.at[q], grecv.at[i, q], g_ss.at[i, j], g_rs.at[i, j], {"tok": p})
                )

        def take_z(j):
            part = zt_f[j, outer, :, :, 0:fz]
            for i in range(n_out - 1):
                za_cp[j, i].wait_recv()
                part = part + zt_r[j, i, :, :, 0:fz].astype(F32)
            zs_f[j, :, :, 0:fz] = part
            zs_b[j, :, :, 0:fz] = part.astype(BF16)
            yb_cp[j] = send(
                zs_b.at[j, across, :, 0:fz], zs_r.at[j, :, 0:fz], yb_ss.at[j], yb_rs.at[j], pair
            )

        def take_pre(f):
            w = fa[f]
            ahead(fa, f).wait_recv()
            g = grad[sect, :, inner].reshape(n_out * sub, width)
            own = jnp.dot(
                g, turned[:, starts[f]:starts[f] + w], preferred_element_type=F32
            ).reshape(n_out, sub, w)
            c = coef[:, inner]
            both = (
                own
                + c[:, :, 2:3] * pre_r[f, 0, :, :, 0:w].astype(F32)
                + c[:, :, 3:4] * pre_r[f, 1, :, :, 0:w].astype(F32)
            )
            pass_on(0, f, both)

        def take_y(j, f):
            w = fa[f]
            ya_cp[j, f].wait_recv()
            pass_on(j, f, yt_f[j, f, :, inner, :, 0:w] + yt_r[j, f, :, :, 0:w].astype(F32))

        def pass_on(j, f, both):
            w = fa[f]
            ys_f[j, f, :, :, 0:w] = both
            ys_b[j, f, :, :, 0:w] = both.astype(BF16)
            for i, p in enumerate(out_peers):
                zb_cp[j, f, i] = send(
                    ys_b.at[j, f, p, :, 0:w], ys_r.at[j, f, i, :, 0:w],
                    zb_ss.at[j, f, i], zb_rs.at[j, f, i], zp[i],
                )

        g_cp, n_cp = [], []
        terms(0, sect)
        o_cp.wait_recv()
        terms(1, oth)
        for f in range(n_pre):
            take_pre(f)
        kl = cross / zt - jnp.log(zt) + jnp.log(zs)
        num[...] = jnp.broadcast_to(jnp.sum(live * kl, axis=1, keepdims=True), num.shape)
        for i, (s, p) in enumerate(sum_peers):
            n_cp.append(send(num, nrecv.at[i], n_ss.at[i], n_rs.at[i], {"sect": s, "tok": p}))
        head_acc[...] = jnp.dot(
            hown[...], grad[...].reshape(rows, width), preferred_element_type=F32
        )
        if late:
            take_z(0)
            y_terms(0, grad[sect].reshape(half, width))
            y_terms(1, grad[oth].reshape(half, width))
            take_z(1)
        for j in range(2):
            for f in range(len(fa)):
                if j or f >= n_pre:
                    take_y(j, f)
                if fz and f == 0 and not late:
                    take_z(j)

        head = head_acc[...]
        numerator = num[...]
        for i, copy in enumerate(n_cp):
            copy.wait_recv()
            numerator = numerator + nrecv[i]
        for i in range(n_tok - 1):
            h_cp[i].wait_recv()
            theirs = hrecv[i].reshape(rows, block).T
            g_cp[i].wait_recv()
            g_cp[n_tok - 1 + i].wait_recv()
            head = head + jnp.dot(
                theirs, grecv[i].reshape(rows, width), preferred_element_type=F32
            )
        head_ref[...] = head.astype(BF16)
        loss_ref[...] = numerator / live_total

        for j, q in ((0, sect), (1, oth)):
            if fz:
                yb_cp[j].wait_recv()
                mine = zs_f[j, inner, :, 0:fz] + zs_r[j, :, 0:fz].astype(F32)
                hid_ref[q, :, 0:fz] = mine.astype(BF16)
            for f, w in enumerate(fa):
                hid = ys_f[j, f, outer, :, 0:w]
                for i in range(n_out - 1):
                    zb_cp[j, f, i].wait_recv()
                    hid = hid + ys_r[j, f, i, :, 0:w].astype(F32)
                hid_ref[q, :, starts[f]:starts[f] + w] = hid.astype(BF16)
        for copy in g_cp + n_cp:
            copy.wait_send()
        for f in range(n_pre):
            ahead(fa, f).wait_send()
        for group in (za_cp, zb_cp, ya_cp, yb_cp):
            for copy in group.values():
                copy.wait_send()

    for core, plan in enumerate(plans):
        pl.when(sect == core)(functools.partial(spread, *plan))
    o_cp.wait_send()
    for copy in p_cp + c_cp + h_cp + s_cp:
        copy.wait_send()


def emit(loss_in, head_in, hid_in, loss_out, head_out, hid_out, sems):
    copies = [
        pltpu.make_async_copy(head_in, head_out, sems.at[0]),
        pltpu.make_async_copy(hid_in, hid_out, sems.at[1]),
    ]
    for copy in copies:
        copy.start()
    loss_out[...] = loss_in[0:1, 0:1]
    for copy in copies:
        copy.wait()


def fused_body(n_tok, n_voc, teacher_hidden, teacher_head, student_hidden, student_head, live_counts):
    rows, t_feats = teacher_hidden.shape
    feats, width = student_head.shape
    kc = t_feats // 4
    third, fourth = feats // 3, feats // 4
    plans = (
        (0, (third,) * 3, 2, False),
        (third, (fourth, feats - third - fourth), 1, True),
    )
    fz = max(plan[0] for plan in plans)
    fw = max(max(plan[1]) for plan in plans)
    ny = max(len(plan[1]) for plan in plans)
    block, out_rows, half = feats // n_tok, rows // n_voc, rows // 2
    sub = out_rows // 2
    n_in, n_out = 2, n_voc // 2
    tp, vp, op, sp = n_tok - 1, n_voc - 1, n_out - 1, 2 * n_tok - 1
    steps = t_feats // kc
    vmem, dma = pltpu.VMEM, pltpu.SemaphoreType.DMA
    any_spec = pl.BlockSpec(memory_space=pl.ANY)
    vm_spec = pl.BlockSpec(memory_space=pltpu.VMEM)
    loss, head, hid = pl.pallas_call(
        functools.partial(fused, n_tok, n_in, n_out, kc, plans),
        out_shape=(
            jax.ShapeDtypeStruct((8, 128), F32),
            jax.ShapeDtypeStruct((block, width), BF16),
            jax.ShapeDtypeStruct((2, sub, feats), BF16),
        ),
        in_specs=[pl.BlockSpec(memory_space=pltpu.SMEM)] + [any_spec] * 4,
        out_specs=(vm_spec,) * 3,
        scratch_shapes=[
            vmem((steps, 2, n_voc, sub, kc), BF16), vmem((steps, kc, width), BF16),
            vmem((2, n_voc, sub, feats), BF16), vmem((feats, width), BF16), vmem((width, feats), BF16),
            vmem((2, half, width), F32), vmem((2, half, width), F32),
            vmem((half, width), F32), vmem((half, width), F32), vmem((half, width), F32),
            vmem((half, width), F32), vmem((half, width), F32),
            vmem((half, 128), F32), vmem((4, half), F32), vmem((vp, 4, half), F32),
            vmem((8, 128), F32), vmem((tp, 8, 128), F32),
            vmem((8, 128), F32), vmem((sp, 8, 128), F32),
            vmem((block, rows), BF16), vmem((tp, 2, n_voc, sub, block), BF16),
            vmem((2, n_out, n_in, sub, width), BF16), vmem((tp, 2, n_out, n_in, sub, width), BF16),
            vmem((block, width), F32),
            vmem((n_out, n_in, sub, 128), F32), vmem((2, n_out, sub, width), BF16),
            vmem((ny, 2, n_out, sub, fw), BF16), vmem((ny, 2, n_out, sub, fw), BF16),
            vmem((2, n_out, n_in, sub, fz), F32), vmem((2, n_out, n_in, sub, fz), BF16),
            vmem((2, op, n_in, sub, fz), BF16),
            vmem((2, n_in, sub, fz), F32), vmem((2, n_in, sub, fz), BF16),
            vmem((2, sub, fz), BF16),
            vmem((2, ny, n_out, n_in, sub, fw), F32), vmem((2, ny, n_out, n_in, sub, fw), BF16),
            vmem((2, ny, n_out, sub, fw), BF16),
            vmem((2, ny, n_out, sub, fw), F32), vmem((2, ny, n_out, sub, fw), BF16),
            vmem((2, ny, op, sub, fw), BF16),
            dma((3 + 3 * steps,)), dma((3,)), dma((3,)), dma((tp,)), dma((tp,)), dma((tp,)), dma((tp,)),
            dma((vp,)), dma((vp,)), dma((tp, 2)), dma((tp, 2)), dma((sp,)), dma((sp,)),
            dma(()), dma(()), dma((2, op)), dma((2, op)), dma((2, ny, op)), dma((2, ny, op)),
            dma((2, ny)), dma((2, ny)), dma((2,)), dma((2,)), dma((ny,)), dma((ny,)),
        ],
        compiler_params=pltpu.CompilerParams(
            collective_id=0, has_side_effects=True, vmem_limit_bytes=53 * 1024 * 1024
        ),
    )(
        live_counts, teacher_hidden.reshape(n_voc, 2, sub, t_feats), teacher_head,
        student_hidden.reshape(n_voc, 2, sub, feats), student_head,
    )
    hid = hid.reshape(out_rows, feats)
    loss, head, hid = pl.pallas_call(
        emit,
        out_shape=(
            jax.ShapeDtypeStruct((1, 1), F32),
            jax.ShapeDtypeStruct(head.shape, BF16),
            jax.ShapeDtypeStruct(hid.shape, BF16),
        ),
        in_specs=[vm_spec, any_spec, any_spec],
        out_specs=(vm_spec, any_spec, any_spec),
        scratch_shapes=[dma((2,))],
        compiler_params=pltpu.CompilerParams(vmem_limit_bytes=4 * 1024 * 1024),
    )(loss, head, hid)
    return (loss[0, 0], head, hid)


def solution(mesh):
    placed = (P("tok", "sect"), P("sect", "vocab"), P("tok", "sect"), P("sect", "vocab"), P("tok"))
    n_tok, n_voc = mesh.shape["tok"], mesh.shape["vocab"]

    def run(*args):
        rows = args[0].shape[0]
        fits = rows == 256 and rows % (TILE * n_voc) == 0 and n_voc % 2 == 0 and n_voc > 2
        fits = fits and args[2].shape[1] % (12 * 128) == 0 and args[2].shape[1] % (128 * n_tok) == 0
        if fits and n_tok > 1:
            return fused_body(n_tok, n_voc, *args)
        return body(*args)

    return jax.shard_map(
        run,
        mesh=mesh,
        in_specs=placed,
        out_specs=(P(), P(("sect", "tok"), "vocab"), P(("tok", "vocab"), "sect")),
        check_vma=False,
    )
```
